32 devices in a mesh: groups: 2 (over x), lon: 16 (over z, y, core).
Axes of the slice: x: 2, y: 2, z: 4, core: 2. Of those that a mesh axis runs over, the one named last changes fastest.
Arguments:
- fields: float32 [6, 128, 2304], P('groups', 'lon'), parts along dimension 0, may hold values from -6 to 6
- shifts: int32 [4608], P('groups'), parts along dimension 0, may hold values from 0 to 24, as said below
- fraction: float32 [4608], P('groups'), parts along dimension 0, may hold values from 0.05 to 0.95
- cutoff: int32 [256], P('groups'), parts along dimension 0, may hold values from 1 to 21, as said below
Outputs:
- transported: float32 [6, 128, 2304], P('groups', 'lon'), parts along dimension 0
The draws below stay inside these ranges and needn't reach their ends.
There are 2 independent parts, one for each index of `groups`. The reference program is written for one: setup_inputs(seed, part) draws one part's arguments, and reference() takes and returns one part's arrays. A program takes and returns all parts, laid end to end along the dimension named above; each array names one. Nothing has to cross between parts.
Inputs may be any that keep to these rules, and one draw needn't show every extreme that they name: `shifts`: rows of the first and last 64 latitudes move by up to 24 cells, and that bound is reached in every draw; every other row moves by at most 5 cells, which is also reached in every draw. The largest cutoff 21 is reached in every draw.
All inputs are finite; a program needn't handle non-finite values.
Results may differ from the reference program's by a relative error of at most 0.00005.
Values sent between devices are 32-bit elements; how exact they have to be, the bound alone decides.
A program may use at most 64 MiB of HBM per device.

```python
import jax
import jax.numpy as jnp
from jax import lax

FIELDS = 3
CL = 8
LATW = 192
LEV = 12
PLAT = 64
NLON = 128
ROWS = 2304
KC = 21


def draw_shifts(key, part):
    row_count = LATW * LEV
    polar_count = PLAT * LEV
    row_number = jnp.arange(row_count, dtype=jnp.int32)
    is_polar = (row_number < polar_count) | (row_number >= row_count - polar_count)
    far_moves = jax.random.randint(jax.random.fold_in(key, 11), (row_count,), 0, 3 * CL + 1)
    near_moves = jax.random.randint(jax.random.fold_in(key, 13), (row_count,), 0, CL - 2)
    far_pick = jax.random.randint(jax.random.fold_in(key, 17), (), 0, 2 * polar_count)
    far_row = jnp.where(far_pick < polar_count, far_pick, far_pick + row_count - 2 * polar_count)
    near_row = jax.random.randint(jax.random.fold_in(key, 19), (), polar_count, row_count - polar_count)
    far_moves = jnp.where(row_number == far_row, 3 * CL, far_moves)
    near_moves = jnp.where(row_number == near_row, CL - 3, near_moves)
    return jnp.where(is_polar, far_moves, near_moves).astype(jnp.int32)


def draw_cutoff(key, part):
    row_count = 2 * PLAT
    values = jax.random.randint(jax.random.fold_in(key, 23), (row_count,), 1, KC + 1)
    top_row = jax.random.randint(jax.random.fold_in(key, 29), (), 0, row_count)
    return jnp.where(jnp.arange(row_count) == top_row, KC, values).astype(jnp.int32)


def shard_levels(rng, shape, shards, low, top_value):
    gain = 1.0
    for position, parts in shards:
        draws = jax.random.uniform(jax.random.fold_in(jax.random.fold_in(rng, 6), position), (parts,), jnp.float32, low / len(shards), top_value / len(shards))
        gain = gain * jnp.repeat(jnp.exp(draws), shape[position] // parts).reshape((-1,) + (1,) * (len(shape) - 1 - position))
    return gain


def noise(stream_key, extent, spread, bound, split=(), held_as=jnp.bfloat16):
    gain = shard_levels(stream_key, extent, split, -0.22, 0.18) if split else 1.0
    drawn = jax.random.normal(stream_key, extent, jnp.float32) * spread * gain
    return jnp.minimum(jnp.maximum(drawn, -bound), bound).astype(held_as)


def setup_inputs(seed: int = 0, part: int = 0) -> dict:
    seeds = jax.random.split(jax.random.key(seed), 5)
    own_keys = jax.random.split(jax.random.fold_in(seeds[4], part), 5)
    fields = noise(own_keys[0], (FIELDS, NLON, ROWS), 1.0, 6.0, ((1, 16),), jnp.float32)
    shifts = draw_shifts(jax.random.fold_in(jax.random.fold_in(seeds[4], part), 71), part)
    fraction = jnp.clip(jax.random.uniform(own_keys[2], (ROWS,), jnp.float32, 0.05, 0.95), 0.05, 0.95)
    cutoff = draw_cutoff(jax.random.fold_in(jax.random.fold_in(seeds[4], part), 71), part)
    return {"fields": fields, "shifts": shifts, "fraction": fraction, "cutoff": cutoff}


def remap_cells(shifted, fraction):
    right_one = jnp.roll(shifted, -1, axis=0)
    right_two = jnp.roll(shifted, -2, axis=0)
    left_one = jnp.roll(shifted, 1, axis=0)
    right_face = (7.0 * (shifted + right_one) - (left_one + right_two)) / 12.0
    left_face = jnp.roll(right_face, 1, axis=0)
    courant = fraction[None, :]
    face_step = right_face - left_face
    curvature = 6.0 * (shifted - 0.5 * (left_face + right_face))
    face_flux = courant * (right_face - 0.5 * courant * (face_step - (1.0 - 2.0 * courant / 3.0) * curvature))
    return shifted - (face_flux - jnp.roll(face_flux, 1, axis=0))


def reference(fields, shifts, fraction, cutoff):
    cycle_cells = fields.shape[1]
    row_count = fields.shape[2]
    polar_count = PLAT * LEV
    positions = jnp.arange(cycle_cells, dtype=jnp.int32)
    source_index = (positions[:, None] - shifts[None, :].astype(jnp.int32)) % cycle_cells
    wave_index = jnp.arange(cycle_cells // 2 + 1, dtype=jnp.int32)
    row_limit = jnp.repeat(cutoff.astype(jnp.int32), LEV)
    kept_waves = wave_index[:, None] < row_limit[None, :]

    def one_field(values):
        shifted = jnp.take_along_axis(values, source_index, axis=0)
        remapped = remap_cells(shifted, fraction)
        outer_rows = jnp.concatenate([remapped[:, :polar_count], remapped[:, row_count - polar_count:]], axis=1)
        spectrum = jnp.fft.rfft(outer_rows, axis=0)
        smooth = jnp.fft.irfft(jnp.where(kept_waves, spectrum, 0.0), n=cycle_cells, axis=0).astype(values.dtype)
        return jnp.concatenate([smooth[:, :polar_count], remapped[:, polar_count:row_count - polar_count], smooth[:, polar_count:]], axis=1)

    return lax.map(one_field, fields)
```

```python
import functools
import math

import jax
import jax.numpy as jnp
import ml_dtypes
import numpy as np
from jax import lax
from jax.experimental import pallas as pl
from jax.experimental.pallas import tpu as pltpu
from jax.sharding import PartitionSpec as P

LEV = 12
PLAT = 64
LANES = 128
NEAR = 5
MESH = pl.DeviceIdType.MESH
HIGHEST = lax.Precision.HIGHEST


def stencil(c):
    m = 1.0 - 2.0 * c / 3.0
    square = c * c
    alpha = c - 0.5 * square - 1.5 * square * m
    beta = 0.5 * square - 1.5 * square * m
    gamma = 3.0 * square * m
    small, large = -1.0 / 12.0, 7.0 / 12.0
    face = {-1: small, 0: large, 1: large, 2: small}
    flux = {}
    for j in range(-2, 3):
        total = None
        for scale, tap in ((alpha, face.get(j)), (beta, face.get(j + 1))):
            if tap is not None:
                total = scale * tap if total is None else total + scale * tap
        flux[j] = total + gamma if j == 0 else total
    taps = {}
    for j in range(-3, 3):
        value = flux[j + 1] if j + 1 in flux else None
        if j in flux:
            value = -flux[j] if value is None else value - flux[j]
        taps[j] = value + 1.0 if j == 0 else value
    return taps


def owner_table(n, tiles):
    return [min(t + 1, tiles - 1) * n // 16 for t in range(tiles)]


def slot_table(owners):
    return [owners[:t].count(device) for t, device in enumerate(owners)]


def body(
    n, polar, waves, fields_ref, shifts_ref, fraction_ref, cutoff_ref, forward_ref, inverse_ref, wave_ref,
    out_ref, circles, filtered, window, edge_out, edge_in, factor, weights,
    shifts_in, fraction_in, cutoff_in, forward_in, inverse_in, wave_in, own, local_sem,
    send_sem, recv_sem, back_send_sem, back_recv_sem, halo_send_sem, halo_recv_sem, near_in,
):
    me = lax.axis_index("lon")
    count, cells, rows = fields_ref.shape
    side = polar // LANES
    tiles = 2 * side
    inner = rows - 2 * polar
    cycle = n * cells
    owners = owner_table(n, tiles)
    slot_of = slot_table(owners)
    slots = max(slot_of) + 1

    def lane_of(tile):
        return tile * LANES + inner if tile >= side else tile * LANES

    def picked(slot, value):
        total = jnp.int32(0)
        for t in range(tiles):
            if slot_of[t] == slot:
                total = jnp.where(me == owners[t], value(t), total)
        return total

    def owns(slot):
        return picked(slot, lambda t: 1) == 1

    def my_lanes(slot):
        return pl.ds(pl.multiple_of(picked(slot, lane_of), LANES), LANES)

    held = sum(picked(slot, lambda t: 1) for slot in range(slots))
    east = jnp.where(me + 1 == n, 0, me + 1)
    west = jnp.where(me == 0, n - 1, me - 1)

    def cell_block(device):
        return pl.ds(pl.multiple_of(device * cells, cells), cells)

    def signal(semaphore, device):
        pl.semaphore_signal(semaphore, inc=1, device_id={"lon": device}, device_id_type=MESH)

    def each(act, where):
        def one(device, carry):
            pl.when(where(device))(lambda: act(device))
            return carry

        lax.fori_loop(0, n, one, 0, unroll=n <= 16)

    barrier = pltpu.get_barrier_semaphore()
    is_owner = owns(0)
    free = [device for device in range(n) if device not in owners]

    def is_free(device):
        return functools.reduce(jnp.logical_or, [device == other for other in free], False)

    pl.when(is_owner)(lambda: each(lambda device: signal(barrier, device), lambda device: device != me))

    @pl.when(jnp.logical_not(is_owner))
    def _():
        pl.when(me < n - 1)(lambda: signal(barrier, me + 1))
        pl.when(me == 0)(lambda: signal(barrier, n - 1))

    heard = n - len(free) - is_owner.astype(jnp.int32)
    heard += jnp.where(jnp.logical_and(me > 0, is_free(me - 1)), 1, 0)
    if 0 in free:
        heard += jnp.where(me == n - 1, 1, 0)

    def local(source, target, slot):
        return pltpu.make_async_copy(source, target, local_sem.at[slot])

    small = [
        local(shifts_ref, shifts_in, 0),
        local(fraction_ref, fraction_in, 1),
        local(cutoff_ref, cutoff_in, 2),
        local(wave_ref, wave_in, 3),
    ]
    large = [local(forward_ref, forward_in, 4), local(inverse_ref, inverse_in, 5)]
    own_inner = local(
        fields_ref.at[:, :, pl.ds(polar, inner)], window.at[:, pl.ds(cells, cells), :], 6
    )
    own_cells = local(fields_ref, own, 7)
    own_cells.start()
    for copy in small + large + [own_inner]:
        copy.start()
    edge_out[...] = jnp.zeros_like(edge_out)
    pl.semaphore_wait(barrier, heard)
    pl.when(me > 0)(lambda: signal(near_in.at[0], me - 1))
    pl.when(me == n - 1)(lambda: signal(near_in.at[1], 0))
    own_cells.wait()

    def send_tile(t):
        lanes = pl.ds(lane_of(t), LANES)
        for f in range(count):
            pltpu.make_async_remote_copy(
                src_ref=own.at[f, :, lanes],
                dst_ref=circles.at[slot_of[t], f, cell_block(me), :],
                send_sem=send_sem,
                recv_sem=recv_sem.at[slot_of[t], f],
                device_id={"lon": owners[t]},
                device_id_type=MESH,
            ).start()

    for t in reversed(range(tiles)):
        pl.when(me != owners[t])(lambda t=t: send_tile(t))
    for slot in range(slots):

        @pl.when(owns(slot))
        def _():
            for f in range(count):
                circles[slot, f, cell_block(me), :] = own[f, :, my_lanes(slot)]

    for copy in small + [own_inner]:
        copy.wait()
    for f in range(count):
        edge_out[2 * f : 2 * f + 2, :] = window[f, cells : cells + 2, :]

    to_east = pltpu.make_async_remote_copy(
        src_ref=own.at[:, :, pl.ds(polar, inner)],
        dst_ref=window.at[:, pl.ds(0, cells), :],
        send_sem=halo_send_sem.at[0],
        recv_sem=halo_recv_sem.at[0],
        device_id={"lon": east},
        device_id_type=MESH,
    )
    to_west = pltpu.make_async_remote_copy(
        src_ref=edge_out,
        dst_ref=edge_in,
        send_sem=halo_send_sem.at[1],
        recv_sem=halo_recv_sem.at[1],
        device_id={"lon": west},
        device_id_type=MESH,
    )

    def send_halo():
        pl.when(me < n - 1)(lambda: pl.semaphore_wait(near_in.at[0], 1))
        to_east.start()
        pl.when(me == 0)(lambda: pl.semaphore_wait(near_in.at[1], 1))
        to_west.start()

    send_halo()
    padded = factor.shape[2]

    for slot in range(slots):

        @pl.when(owns(slot))
        def _():
            my_tile = picked(slot, lambda t: t)
            my_row = picked(slot, lambda t: lane_of(t) // LANES)
            c = fraction_in[pl.ds(my_row, 1), :]
            o = stencil(c)
            column = [wave_in[:, m : m + 1] for m in range(8)]
            cos1, cos2, cos3, sin1, sin2, sin3, weight, number = column
            real = o[0] + (o[1] + o[-1]) * cos1 + (o[2] + o[-2]) * cos2 + o[-3] * cos3
            imag = (o[1] - o[-1]) * sin1 + (o[2] - o[-2]) * sin2 - o[-3] * sin3
            turns = number * (shifts_in[pl.ds(my_row, 1), :].astype(jnp.float32) * (1.0 / cycle))
            angle = (turns - jnp.floor(turns)) * (2.0 * math.pi)
            cos_shift = jnp.cos(angle)
            sin_shift = jnp.sin(angle)
            latitudes = cutoff_in.shape[1]
            first = lax.broadcasted_iota(jnp.int32, (latitudes, LANES), 0) * LEV
            row = lax.broadcasted_iota(jnp.int32, (latitudes, LANES), 1) + my_tile * LANES
            chosen = jnp.where((row >= first) & (row < first + LEV), 1.0, 0.0)
            limits = jnp.broadcast_to(cutoff_in[...].astype(jnp.float32), (8, latitudes))
            limit = jnp.dot(limits, chosen, precision=HIGHEST, preferred_element_type=jnp.float32)
            kept = jnp.where(number + 0.5 < limit[0:1], weight, 0.0)
            factor[slot, 0] = kept * (cos_shift * real + sin_shift * imag)
            factor[slot, 1] = kept * (cos_shift * imag - sin_shift * real)

    inner_rows = slice(side, side + inner // LANES)
    inner_taps = stencil(fraction_in[inner_rows, :])
    moves = shifts_in[inner_rows, :]
    is_move = [moves == s for s in range(NEAR + 1)]
    for t in range(-3 - NEAR, 3):
        total = jnp.zeros_like(inner_taps[0])
        for s in range(NEAR + 1):
            if -3 <= t + s <= 2:
                total = jnp.where(is_move[s], inner_taps[t + s], total)
        weights[t + 3 + NEAR] = total
    for copy in large:
        copy.wait()

    def drain(ref, semaphore):
        pltpu.make_async_copy(ref, ref, semaphore).wait()

    for f in range(count):
        for slot in range(slots):

            @pl.when(owns(slot))
            def _():
                lanes = my_lanes(slot)
                drain(circles.at[slot, f, pl.ds(0, (n - 1) * cells), :], recv_sem.at[slot, f])
                spectrum = jnp.dot(
                    forward_in[...], triple(circles[slot, f]), preferred_element_type=jnp.float32
                )
                p, q = factor[slot, 0], factor[slot, 1]
                a, b = spectrum[:padded], spectrum[padded:]
                scaled = jnp.concatenate([a * p + b * q, b * p - a * q], axis=0)
                filtered[slot, f] = jnp.dot(
                    inverse_in[...], triple(scaled), preferred_element_type=jnp.float32
                )

                def send_back(device):
                    pltpu.make_async_remote_copy(
                        src_ref=filtered.at[slot, f, cell_block(device), :],
                        dst_ref=out_ref.at[f, :, lanes],
                        send_sem=back_send_sem,
                        recv_sem=back_recv_sem,
                        device_id={"lon": device},
                        device_id_type=MESH,
                    ).start()

                each(send_back, lambda device: device != me)
                out_ref[f, :, lanes] = filtered[slot, f, cell_block(me), :]

    to_east.wait_recv()
    to_west.wait_recv()
    for f in range(count):
        window[f, 2 * cells : 2 * cells + 2, :] = edge_in[2 * f : 2 * f + 2, :]
    for block in range(inner // LANES):
        lanes = slice(block * LANES, (block + 1) * LANES)
        tap = [
            jnp.broadcast_to(weights[m, block : block + 1, :], (cells, LANES)) for m in range(6 + NEAR)
        ]
        for f in range(count):
            total = None
            for m in range(6 + NEAR):
                start = cells + m - 3 - NEAR
                term = tap[m] * window[f, start : start + cells, lanes]
                total = term if total is None else total + term
            out_ref[f, :, polar + block * LANES : polar + (block + 1) * LANES] = total

    to_east.wait_send()
    to_west.wait_send()
    for k in range(slots + 1):

        @pl.when(held == k)
        def _():
            others = out_ref.at[:, :, pl.ds(0, (tiles - k) * LANES)]
            drain(others, send_sem)
            drain(others, back_recv_sem)
            for slot in range(k):
                drain(filtered.at[slot, :, pl.ds(0, (n - 1) * cells), :], back_send_sem)


def halves(values):
    high = values.astype(jnp.bfloat16)
    return high, (values - high.astype(jnp.float32)).astype(jnp.bfloat16)


def triple(values):
    high, low = halves(values)
    return jnp.concatenate([high, low, high], axis=0)


def tables(cycle, waves, padded):
    wave = np.arange(padded)
    phase = 2.0 * np.pi / cycle * (np.arange(cycle)[None, :] * wave[:, None] % cycle)
    live = (wave < waves)[:, None]
    forward = np.concatenate([np.cos(phase) * live, np.sin(phase) * live], axis=0)
    theta = 2.0 * np.pi / cycle * wave
    weight = np.where(wave == 0, 1.0, 2.0) / cycle * (wave < waves)
    columns = [np.cos(theta), np.cos(2 * theta), np.cos(3 * theta)]
    columns += [np.sin(theta), np.sin(2 * theta), np.sin(3 * theta), weight, wave]
    per_wave = np.stack(columns, axis=1)
    def stacked(matrix):
        high = matrix.astype(ml_dtypes.bfloat16)
        low = (matrix - high.astype(np.float64)).astype(ml_dtypes.bfloat16)
        return np.concatenate([high, high, low], axis=1)

    return stacked(forward), stacked(forward.T), per_wave.astype(np.float32)


def shards(fields, shifts, fraction, cutoff):
    n = lax.axis_size("lon")
    count, cells, rows = fields.shape
    polar = PLAT * LEV
    inner = rows - 2 * polar
    tiles = 2 * polar // LANES
    cycle = cells * n
    waves = cycle // 6
    slots = max(slot_table(owner_table(n, tiles))) + 1
    padded = -(-waves // 8) * 8
    forward, inverse, per_wave = tables(cycle, waves, padded)
    operands = [fields, shifts.reshape(-1, LANES), fraction.reshape(-1, LANES), cutoff[None]]
    operands += [jnp.asarray(x) for x in (forward, inverse, per_wave)]
    vmem = pl.BlockSpec(memory_space=pltpu.VMEM)
    f32 = jnp.float32
    return pl.pallas_call(
        functools.partial(body, n, polar, waves),
        out_shape=pltpu.VMEM(fields.shape, f32),
        in_specs=[pl.BlockSpec(memory_space=pltpu.HBM)] * 7,
        out_specs=vmem,
        scratch_shapes=[
            pltpu.VMEM((slots, count, cycle, LANES), f32),
            pltpu.VMEM((slots, count, cycle, LANES), f32),
            pltpu.VMEM((count, 3 * cells, inner), f32),
            pltpu.VMEM((8, inner), f32),
            pltpu.VMEM((8, inner), f32),
            pltpu.VMEM((slots, 2, padded, LANES), f32),
            pltpu.VMEM((6 + NEAR, inner // LANES, LANES), f32),
            pltpu.VMEM((rows // LANES, LANES), jnp.int32),
            pltpu.VMEM((rows // LANES, LANES), f32),
            pltpu.VMEM((1, cutoff.shape[0]), jnp.int32),
            pltpu.VMEM(forward.shape, jnp.bfloat16),
            pltpu.VMEM(inverse.shape, jnp.bfloat16),
            pltpu.VMEM(per_wave.shape, f32),
            pltpu.VMEM(fields.shape, f32),
            pltpu.SemaphoreType.DMA((8,)),
            pltpu.SemaphoreType.DMA,
            pltpu.SemaphoreType.DMA((slots, count)),
            pltpu.SemaphoreType.DMA,
            pltpu.SemaphoreType.DMA,
            pltpu.SemaphoreType.DMA((2,)),
            pltpu.SemaphoreType.DMA((2,)),
            pltpu.SemaphoreType.REGULAR((2,)),
        ],
        compiler_params=pltpu.CompilerParams(
            collective_id=0, has_side_effects=True, vmem_limit_bytes=32 * 1024 * 1024
        ),
        name="zonal",
    )(*[pltpu.with_memory_space_constraint(x, pltpu.HBM) for x in operands])


def solution(mesh):
    placed = (P("groups", "lon", None), P("groups"), P("groups"), P("groups"))
    return jax.shard_map(
        shards, mesh=mesh, in_specs=placed, out_specs=P("groups", "lon", None), check_vma=False
    )
```

```python
import functools
import math

import jax
import jax.numpy as jnp
import ml_dtypes
import numpy as np
from jax import lax
from jax.experimental import pallas as pl
from jax.experimental.pallas import tpu as pltpu
from jax.sharding import PartitionSpec as P

LEV = 12
PLAT = 64
LANES = 128
NEAR = 5
MESH = pl.DeviceIdType.MESH
HIGHEST = lax.Precision.HIGHEST


def stencil(c):
    m = 1.0 - 2.0 * c / 3.0
    square = c * c
    alpha = c - 0.5 * square - 1.5 * square * m
    beta = 0.5 * square - 1.5 * square * m
    gamma = 3.0 * square * m
    small, large = -1.0 / 12.0, 7.0 / 12.0
    face = {-1: small, 0: large, 1: large, 2: small}
    flux = {}
    for j in range(-2, 3):
        total = None
        for scale, tap in ((alpha, face.get(j)), (beta, face.get(j + 1))):
            if tap is not None:
                total = scale * tap if total is None else total + scale * tap
        flux[j] = total + gamma if j == 0 else total
    taps = {}
    for j in range(-3, 3):
        value = flux[j + 1] if j + 1 in flux else None
        if j in flux:
            value = -flux[j] if value is None else value - flux[j]
        taps[j] = value + 1.0 if j == 0 else value
    return taps


def owner_table(n, tiles):
    return [min(t + 1, tiles - 1) * n // 16 for t in range(tiles)]


def slot_table(owners):
    return [owners[:t].count(device) for t, device in enumerate(owners)]


def body(
    n, polar, waves, fields_ref, shifts_ref, fraction_ref, cutoff_ref, forward_ref, inverse_ref, wave_ref,
    out_ref, circles, filtered, window, edge_out, edge_in, factor, weights,
    shifts_in, fraction_in, cutoff_in, forward_in, inverse_in, wave_in, own, local_sem,
    send_sem, recv_sem, back_send_sem, back_recv_sem, halo_send_sem, halo_recv_sem, near_in,
):
    me = lax.axis_index("lon")
    count, cells, rows = fields_ref.shape
    side = polar // LANES
    tiles = 2 * side
    inner = rows - 2 * polar
    cycle = n * cells
    owners = owner_table(n, tiles)
    slot_of = slot_table(owners)
    slots = max(slot_of) + 1

    def lane_of(tile):
        return tile * LANES + inner if tile >= side else tile * LANES

    def picked(slot, value):
        total = jnp.int32(0)
        for t in range(tiles):
            if slot_of[t] == slot:
                total = jnp.where(me == owners[t], value(t), total)
        return total

    def owns(slot):
        return picked(slot, lambda t: 1) == 1

    def my_lanes(slot):
        return pl.ds(pl.multiple_of(picked(slot, lane_of), LANES), LANES)

    held = sum(picked(slot, lambda t: 1) for slot in range(slots))
    east = jnp.where(me + 1 == n, 0, me + 1)
    west = jnp.where(me == 0, n - 1, me - 1)

    def cell_block(device):
        return pl.ds(pl.multiple_of(device * cells, cells), cells)

    def signal(semaphore, device):
        pl.semaphore_signal(semaphore, inc=1, device_id={"lon": device}, device_id_type=MESH)

    def each(act, where):
        def one(device, carry):
            pl.when(where(device))(lambda: act(device))
            return carry

        lax.fori_loop(0, n, one, 0, unroll=n <= 16)

    barrier = pltpu.get_barrier_semaphore()
    is_owner = owns(0)
    free = [device for device in range(n) if device not in owners]

    def is_free(device):
        return functools.reduce(jnp.logical_or, [device == other for other in free], False)

    pl.when(is_owner)(lambda: each(lambda device: signal(barrier, device), lambda device: device != me))

    @pl.when(jnp.logical_not(is_owner))
    def _():
        pl.when(me < n - 1)(lambda: signal(barrier, me + 1))
        pl.when(me == 0)(lambda: signal(barrier, n - 1))

    heard = n - len(free) - is_owner.astype(jnp.int32)
    heard += jnp.where(jnp.logical_and(me > 0, is_free(me - 1)), 1, 0)
    if 0 in free:
        heard += jnp.where(me == n - 1, 1, 0)

    def local(source, target, slot):
        return pltpu.make_async_copy(source, target, local_sem.at[slot])

    small = [
        local(shifts_ref, shifts_in, 0),
        local(fraction_ref, fraction_in, 1),
        local(cutoff_ref, cutoff_in, 2),
        local(wave_ref, wave_in, 3),
    ]
    large = [local(forward_ref, forward_in, 4), local(inverse_ref, inverse_in, 5)]
    own_inner = local(
        fields_ref.at[:, :, pl.ds(polar, inner)], window.at[:, pl.ds(cells, cells), :], 6
    )
    own_cells = local(fields_ref, own, 7)
    own_cells.start()
    for copy in small + large + [own_inner]:
        copy.start()
    edge_out[...] = jnp.zeros_like(edge_out)
    pl.semaphore_wait(barrier, heard)
    pl.when(me > 0)(lambda: signal(near_in.at[0], me - 1))
    pl.when(me == n - 1)(lambda: signal(near_in.at[1], 0))
    own_cells.wait()

    def send_tile(t):
        lanes = pl.ds(lane_of(t), LANES)
        pltpu.make_async_remote_copy(
            src_ref=own.at[:, :, lanes],
            dst_ref=circles.at[slot_of[t], :, cell_block(me), :],
            send_sem=send_sem,
            recv_sem=recv_sem.at[slot_of[t], 0],
            device_id={"lon": owners[t]},
            device_id_type=MESH,
        ).start()

    for t in reversed(range(tiles)):
        pl.when(me != owners[t])(lambda t=t: send_tile(t))
    for slot in range(slots):

        @pl.when(owns(slot))
        def _():
            for f in range(count):
                circles[slot, f, cell_block(me), :] = own[f, :, my_lanes(slot)]

    for copy in small + [own_inner]:
        copy.wait()
    for f in range(count):
        edge_out[2 * f : 2 * f + 2, :] = window[f, cells : cells + 2, :]

    to_east = pltpu.make_async_remote_copy(
        src_ref=own.at[:, :, pl.ds(polar, inner)],
        dst_ref=window.at[:, pl.ds(0, cells), :],
        send_sem=halo_send_sem.at[0],
        recv_sem=halo_recv_sem.at[0],
        device_id={"lon": east},
        device_id_type=MESH,
    )
    to_west = pltpu.make_async_remote_copy(
        src_ref=edge_out,
        dst_ref=edge_in,
        send_sem=halo_send_sem.at[1],
        recv_sem=halo_recv_sem.at[1],
        device_id={"lon": west},
        device_id_type=MESH,
    )

    def send_halo():
        pl.when(me < n - 1)(lambda: pl.semaphore_wait(near_in.at[0], 1))
        to_east.start()
        pl.when(me == 0)(lambda: pl.semaphore_wait(near_in.at[1], 1))
        to_west.start()

    send_halo()
    padded = factor.shape[2]

    for slot in range(slots):

        @pl.when(owns(slot))
        def _():
            my_tile = picked(slot, lambda t: t)
            my_row = picked(slot, lambda t: lane_of(t) // LANES)
            c = fraction_in[pl.ds(my_row, 1), :]
            o = stencil(c)
            column = [wave_in[:, m : m + 1] for m in range(8)]
            cos1, cos2, cos3, sin1, sin2, sin3, weight, number = column
            real = o[0] + (o[1] + o[-1]) * cos1 + (o[2] + o[-2]) * cos2 + o[-3] * cos3
            imag = (o[1] - o[-1]) * sin1 + (o[2] - o[-2]) * sin2 - o[-3] * sin3
            turns = number * (shifts_in[pl.ds(my_row, 1), :].astype(jnp.float32) * (1.0 / cycle))
            angle = (turns - jnp.floor(turns)) * (2.0 * math.pi)
            cos_shift = jnp.cos(angle)
            sin_shift = jnp.sin(angle)
            latitudes = cutoff_in.shape[1]
            first = lax.broadcasted_iota(jnp.int32, (latitudes, LANES), 0) * LEV
            row = lax.broadcasted_iota(jnp.int32, (latitudes, LANES), 1) + my_tile * LANES
            chosen = jnp.where((row >= first) & (row < first + LEV), 1.0, 0.0)
            limits = jnp.broadcast_to(cutoff_in[...].astype(jnp.float32), (8, latitudes))
            limit = jnp.dot(limits, chosen, precision=HIGHEST, preferred_element_type=jnp.float32)
            kept = jnp.where(number + 0.5 < limit[0:1], weight, 0.0)
            factor[slot, 0] = kept * (cos_shift * real + sin_shift * imag)
            factor[slot, 1] = kept * (cos_shift * imag - sin_shift * real)

    inner_rows = slice(side, side + inner // LANES)
    inner_taps = stencil(fraction_in[inner_rows, :])
    moves = shifts_in[inner_rows, :]
    is_move = [moves == s for s in range(NEAR + 1)]
    for t in range(-3 - NEAR, 3):
        total = jnp.zeros_like(inner_taps[0])
        for s in range(NEAR + 1):
            if -3 <= t + s <= 2:
                total = jnp.where(is_move[s], inner_taps[t + s], total)
        weights[t + 3 + NEAR] = total
    for copy in large:
        copy.wait()

    def at(place):
        side, rest = lax.div(place, n // 2), lax.rem(place, n // 2)
        return lax.div(rest, 2) * 4 + side * 2 + lax.rem(rest, 2)

    def drain(ref, semaphore):
        pltpu.make_async_copy(ref, ref, semaphore).wait()

    for slot in reversed(range(slots)):

        @pl.when(owns(slot))
        def _():
            lanes = my_lanes(slot)
            drain(circles.at[slot, :, pl.ds(0, (n - 1) * cells), :], recv_sem.at[slot, 0])
            whole = jnp.concatenate([circles[slot, f] for f in range(count)], axis=1)
            spectrum = jnp.dot(forward_in[...], triple(whole), preferred_element_type=jnp.float32)
            p = jnp.concatenate([factor[slot, 0]] * count, axis=1)
            q = jnp.concatenate([factor[slot, 1]] * count, axis=1)
            a, b = spectrum[:padded], spectrum[padded:]
            scaled = jnp.concatenate([a * p + b * q, b * p - a * q], axis=0)
            smooth = jnp.dot(inverse_in[...], triple(scaled), preferred_element_type=jnp.float32)
            for f in range(count):
                filtered[slot, f] = smooth[:, f * LANES : (f + 1) * LANES]

            def send_back(device):
                pltpu.make_async_remote_copy(
                    src_ref=filtered.at[slot, :, cell_block(device), :],
                    dst_ref=out_ref.at[:, :, lanes],
                    send_sem=back_send_sem,
                    recv_sem=back_recv_sem,
                    device_id={"lon": device},
                    device_id_type=MESH,
                ).start()

            each(lambda place: send_back(at(place)), lambda place: at(place) != me)
            out_ref[:, :, lanes] = filtered[slot, :, cell_block(me), :]

    to_east.wait_recv()
    to_west.wait_recv()
    for f in range(count):
        window[f, 2 * cells : 2 * cells + 2, :] = edge_in[2 * f : 2 * f + 2, :]
    for block in range(inner // LANES):
        lanes = slice(block * LANES, (block + 1) * LANES)
        tap = [
            jnp.broadcast_to(weights[m, block : block + 1, :], (cells, LANES)) for m in range(6 + NEAR)
        ]
        for f in range(count):
            total = None
            for m in range(6 + NEAR):
                start = cells + m - 3 - NEAR
                term = tap[m] * window[f, start : start + cells, lanes]
                total = term if total is None else total + term
            out_ref[f, :, polar + block * LANES : polar + (block + 1) * LANES] = total

    to_east.wait_send()
    to_west.wait_send()
    for k in range(slots + 1):

        @pl.when(held == k)
        def _():
            others = out_ref.at[:, :, pl.ds(0, (tiles - k) * LANES)]
            drain(others, send_sem)
            drain(others, back_recv_sem)
            for slot in range(k):
                drain(filtered.at[slot, :, pl.ds(0, (n - 1) * cells), :], back_send_sem)


def halves(values):
    high = values.astype(jnp.bfloat16)
    return high, (values - high.astype(jnp.float32)).astype(jnp.bfloat16)


def triple(values):
    high, low = halves(values)
    return jnp.concatenate([high, low, high], axis=0)


def tables(cycle, waves, padded):
    wave = np.arange(padded)
    phase = 2.0 * np.pi / cycle * (np.arange(cycle)[None, :] * wave[:, None] % cycle)
    live = (wave < waves)[:, None]
    forward = np.concatenate([np.cos(phase) * live, np.sin(phase) * live], axis=0)
    theta = 2.0 * np.pi / cycle * wave
    weight = np.where(wave == 0, 1.0, 2.0) / cycle * (wave < waves)
    columns = [np.cos(theta), np.cos(2 * theta), np.cos(3 * theta)]
    columns += [np.sin(theta), np.sin(2 * theta), np.sin(3 * theta), weight, wave]
    per_wave = np.stack(columns, axis=1)
    def stacked(matrix):
        high = matrix.astype(ml_dtypes.bfloat16)
        low = (matrix - high.astype(np.float64)).astype(ml_dtypes.bfloat16)
        return np.concatenate([high, high, low], axis=1)

    return stacked(forward), stacked(forward.T), per_wave.astype(np.float32)


def shards(fields, shifts, fraction, cutoff):
    n = lax.axis_size("lon")
    count, cells, rows = fields.shape
    polar = PLAT * LEV
    inner = rows - 2 * polar
    tiles = 2 * polar // LANES
    cycle = cells * n
    waves = cycle // 6
    slots = max(slot_table(owner_table(n, tiles))) + 1
    padded = -(-waves // 8) * 8
    forward, inverse, per_wave = tables(cycle, waves, padded)
    operands = [fields, shifts.reshape(-1, LANES), fraction.reshape(-1, LANES), cutoff[None]]
    operands += [jnp.asarray(x) for x in (forward, inverse, per_wave)]
    vmem = pl.BlockSpec(memory_space=pltpu.VMEM)
    f32 = jnp.float32
    return pl.pallas_call(
        functools.partial(body, n, polar, waves),
        out_shape=pltpu.VMEM(fields.shape, f32),
        in_specs=[pl.BlockSpec(memory_space=pltpu.HBM)] * 7,
        out_specs=vmem,
        scratch_shapes=[
            pltpu.VMEM((slots, count, cycle, LANES), f32),
            pltpu.VMEM((slots, count, cycle, LANES), f32),
            pltpu.VMEM((count, 3 * cells, inner), f32),
            pltpu.VMEM((8, inner), f32),
            pltpu.VMEM((8, inner), f32),
            pltpu.VMEM((slots, 2, padded, LANES), f32),
            pltpu.VMEM((6 + NEAR, inner // LANES, LANES), f32),
            pltpu.VMEM((rows // LANES, LANES), jnp.int32),
            pltpu.VMEM((rows // LANES, LANES), f32),
            pltpu.VMEM((1, cutoff.shape[0]), jnp.int32),
            pltpu.VMEM(forward.shape, jnp.bfloat16),
            pltpu.VMEM(inverse.shape, jnp.bfloat16),
            pltpu.VMEM(per_wave.shape, f32),
            pltpu.VMEM(fields.shape, f32),
            pltpu.SemaphoreType.DMA((8,)),
            pltpu.SemaphoreType.DMA,
            pltpu.SemaphoreType.DMA((slots, count)),
            pltpu.SemaphoreType.DMA,
            pltpu.SemaphoreType.DMA,
            pltpu.SemaphoreType.DMA((2,)),
            pltpu.SemaphoreType.DMA((2,)),
            pltpu.SemaphoreType.REGULAR((2,)),
        ],
        compiler_params=pltpu.CompilerParams(
            collective_id=0, has_side_effects=True, vmem_limit_bytes=32 * 1024 * 1024
        ),
        name="zonal",
    )(*[pltpu.with_memory_space_constraint(x, pltpu.HBM) for x in operands])


def solution(mesh):
    placed = (P("groups", "lon", None), P("groups"), P("groups"), P("groups"))
    return jax.shard_map(
        shards, mesh=mesh, in_specs=placed, out_specs=P("groups", "lon", None), check_vma=False
    )
```

```python
import functools
import math

import jax
import jax.numpy as jnp
import ml_dtypes
import numpy as np
from jax import lax
from jax.experimental import pallas as pl
from jax.experimental.pallas import tpu as pltpu
from jax.sharding import PartitionSpec as P

LEV = 12
PLAT = 64
LANES = 128
WEST = (11, 8, 9, 7, 10, 6, 4, 5, 3, 2, 1, 0)
EAST = (6, 2, 11, 5, 1, 9, 8, 4, 10, 7, 3, 0)
NEAR = 5
MESH = pl.DeviceIdType.MESH
HIGHEST = lax.Precision.HIGHEST


def stencil(c):
    m = 1.0 - 2.0 * c / 3.0
    square = c * c
    alpha = c - 0.5 * square - 1.5 * square * m
    beta = 0.5 * square - 1.5 * square * m
    gamma = 3.0 * square * m
    small, large = -1.0 / 12.0, 7.0 / 12.0
    face = {-1: small, 0: large, 1: large, 2: small}
    flux = {}
    for j in range(-2, 3):
        total = None
        for scale, tap in ((alpha, face.get(j)), (beta, face.get(j + 1))):
            if tap is not None:
                total = scale * tap if total is None else total + scale * tap
        flux[j] = total + gamma if j == 0 else total
    taps = {}
    for j in range(-3, 3):
        value = flux[j + 1] if j + 1 in flux else None
        if j in flux:
            value = -flux[j] if value is None else value - flux[j]
        taps[j] = value + 1.0 if j == 0 else value
    return taps


def owner_table(n, tiles):
    return [min(t + 1, tiles - 1) * n // 16 for t in range(tiles)]


def slot_table(owners):
    return [owners[:t].count(device) for t, device in enumerate(owners)]


def body(
    n, polar, waves, fields_ref, shifts_ref, fraction_ref, cutoff_ref, forward_ref, inverse_ref, wave_ref,
    out_ref, circles, filtered, window, edge_out, edge_in, factor, weights,
    shifts_in, fraction_in, cutoff_in, forward_in, inverse_in, wave_in, own, local_sem,
    send_sem, recv_sem, back_send_sem, back_recv_sem, halo_send_sem, halo_recv_sem, near_in,
):
    me = lax.axis_index("lon")
    count, cells, rows = fields_ref.shape
    side = polar // LANES
    tiles = 2 * side
    inner = rows - 2 * polar
    cycle = n * cells
    owners = owner_table(n, tiles)
    slot_of = slot_table(owners)
    slots = max(slot_of) + 1

    def lane_of(tile):
        return tile * LANES + inner if tile >= side else tile * LANES

    def picked(slot, value):
        total = jnp.int32(0)
        for t in range(tiles):
            if slot_of[t] == slot:
                total = jnp.where(me == owners[t], value(t), total)
        return total

    def owns(slot):
        return picked(slot, lambda t: 1) == 1

    def my_lanes(slot):
        return pl.ds(pl.multiple_of(picked(slot, lane_of), LANES), LANES)

    held = sum(picked(slot, lambda t: 1) for slot in range(slots))
    east = jnp.where(me + 1 == n, 0, me + 1)
    west = jnp.where(me == 0, n - 1, me - 1)

    def cell_block(device):
        return pl.ds(pl.multiple_of(device * cells, cells), cells)

    def signal(semaphore, device):
        pl.semaphore_signal(semaphore, inc=1, device_id={"lon": device}, device_id_type=MESH)

    def each(act, where):
        def one(device, carry):
            pl.when(where(device))(lambda: act(device))
            return carry

        lax.fori_loop(0, n, one, 0, unroll=n <= 16)

    own_cells = pltpu.make_async_copy(fields_ref, own, local_sem.at[7])
    own_cells.start()
    barrier = pltpu.get_barrier_semaphore()
    is_owner = owns(0)
    free = [device for device in range(n) if device not in owners]

    def is_free(device):
        return functools.reduce(jnp.logical_or, [device == other for other in free], False)

    pl.when(is_owner)(lambda: each(lambda device: signal(barrier, device), lambda device: device != me))

    @pl.when(jnp.logical_not(is_owner))
    def _():
        pl.when(me < n - 1)(lambda: signal(barrier, me + 1))
        pl.when(me == 0)(lambda: signal(barrier, n - 1))

    heard = n - len(free) - is_owner.astype(jnp.int32)
    heard += jnp.where(jnp.logical_and(me > 0, is_free(me - 1)), 1, 0)
    if 0 in free:
        heard += jnp.where(me == n - 1, 1, 0)

    def local(source, target, slot):
        return pltpu.make_async_copy(source, target, local_sem.at[slot])

    small = [
        local(shifts_ref, shifts_in, 0),
        local(fraction_ref, fraction_in, 1),
        local(cutoff_ref, cutoff_in, 2),
        local(wave_ref, wave_in, 3),
    ]
    large = [local(forward_ref, forward_in, 4), local(inverse_ref, inverse_in, 5)]
    own_inner = local(
        fields_ref.at[:, :, pl.ds(polar, inner)], window.at[:, pl.ds(cells, cells), :], 6
    )
    for copy in small + large + [own_inner]:
        copy.start()
    edge_out[...] = jnp.zeros_like(edge_out)
    pl.semaphore_wait(barrier, heard)
    pl.when(me > 0)(lambda: signal(near_in.at[0], me - 1))
    pl.when(me == n - 1)(lambda: signal(near_in.at[1], 0))
    own_cells.wait()

    def send_tile(t):
        lanes = pl.ds(lane_of(t), LANES)
        pltpu.make_async_remote_copy(
            src_ref=own.at[:, :, lanes],
            dst_ref=circles.at[slot_of[t], :, cell_block(me), :],
            send_sem=send_sem,
            recv_sem=recv_sem.at[slot_of[t], 0],
            device_id={"lon": owners[t]},
            device_id_type=MESH,
        ).start()

    for half, order in enumerate((WEST, EAST)):

        @pl.when(lax.div(me * 2, n) == half)
        def _():
            for t in order if len(order) == tiles else range(tiles):
                pl.when(me != owners[t])(lambda t=t: send_tile(t))

    for slot in range(slots):

        @pl.when(owns(slot))
        def _():
            for f in range(count):
                circles[slot, f, cell_block(me), :] = own[f, :, my_lanes(slot)]

    for copy in small + [own_inner]:
        copy.wait()
    for f in range(count):
        edge_out[2 * f : 2 * f + 2, :] = window[f, cells : cells + 2, :]

    to_east = pltpu.make_async_remote_copy(
        src_ref=own.at[:, :, pl.ds(polar, inner)],
        dst_ref=window.at[:, pl.ds(0, cells), :],
        send_sem=halo_send_sem.at[0],
        recv_sem=halo_recv_sem.at[0],
        device_id={"lon": east},
        device_id_type=MESH,
    )
    to_west = pltpu.make_async_remote_copy(
        src_ref=edge_out,
        dst_ref=edge_in,
        send_sem=halo_send_sem.at[1],
        recv_sem=halo_recv_sem.at[1],
        device_id={"lon": west},
        device_id_type=MESH,
    )

    far = me == n - 1
    pl.when(me < n - 1)(lambda: pl.semaphore_wait(near_in.at[0], 1))
    pl.when(jnp.logical_not(far))(to_east.start)
    pl.when(me == 0)(lambda: pl.semaphore_wait(near_in.at[1], 1))
    to_west.start()

    padded = factor.shape[2]

    for slot in range(slots):

        @pl.when(owns(slot))
        def _():
            my_tile = picked(slot, lambda t: t)
            my_row = picked(slot, lambda t: lane_of(t) // LANES)
            c = fraction_in[pl.ds(my_row, 1), :]
            o = stencil(c)
            column = [wave_in[:, m : m + 1] for m in range(8)]
            cos1, cos2, cos3, sin1, sin2, sin3, weight, number = column
            real = o[0] + (o[1] + o[-1]) * cos1 + (o[2] + o[-2]) * cos2 + o[-3] * cos3
            imag = (o[1] - o[-1]) * sin1 + (o[2] - o[-2]) * sin2 - o[-3] * sin3
            turns = number * (shifts_in[pl.ds(my_row, 1), :].astype(jnp.float32) * (1.0 / cycle))
            angle = (turns - jnp.floor(turns)) * (2.0 * math.pi)
            cos_shift = jnp.cos(angle)
            sin_shift = jnp.sin(angle)
            latitudes = cutoff_in.shape[1]
            first = lax.broadcasted_iota(jnp.int32, (latitudes, LANES), 0) * LEV
            row = lax.broadcasted_iota(jnp.int32, (latitudes, LANES), 1) + my_tile * LANES
            chosen = jnp.where((row >= first) & (row < first + LEV), 1.0, 0.0)
            limits = jnp.broadcast_to(cutoff_in[...].astype(jnp.float32), (8, latitudes))
            limit = jnp.dot(limits, chosen, precision=HIGHEST, preferred_element_type=jnp.float32)
            kept = jnp.where(number + 0.5 < limit[0:1], weight, 0.0)
            factor[slot, 0] = kept * (cos_shift * real + sin_shift * imag)
            factor[slot, 1] = kept * (cos_shift * imag - sin_shift * real)

    inner_rows = slice(side, side + inner // LANES)
    inner_taps = stencil(fraction_in[inner_rows, :])
    moves = shifts_in[inner_rows, :]
    is_move = [moves == s for s in range(NEAR + 1)]
    for t in range(-3 - NEAR, 3):
        total = jnp.zeros_like(inner_taps[0])
        for s in range(NEAR + 1):
            if -3 <= t + s <= 2:
                total = jnp.where(is_move[s], inner_taps[t + s], total)
        weights[t + 3 + NEAR] = total
    for copy in large:
        copy.wait()

    def at(place):
        side, rest = lax.div(place, n // 2), lax.rem(place, n // 2)
        return lax.div(rest, 2) * 4 + side * 2 + lax.rem(rest, 2)

    def drain(ref, semaphore):
        pltpu.make_async_copy(ref, ref, semaphore).wait()

    @pl.when(held == 0)
    def _():
        drain(out_ref.at[:, :, pl.ds(0, tiles * LANES)], send_sem)
        pl.when(far)(to_east.start)

    for slot in reversed(range(slots)):

        @pl.when(owns(slot))
        def _():
            lanes = my_lanes(slot)
            drain(circles.at[slot, :, pl.ds(0, (n - 1) * cells), :], recv_sem.at[slot, 0])
            whole = jnp.concatenate([circles[slot, f] for f in range(count)], axis=1)
            spectrum = jnp.dot(forward_in[...], triple(whole), preferred_element_type=jnp.float32)
            p = jnp.concatenate([factor[slot, 0]] * count, axis=1)
            q = jnp.concatenate([factor[slot, 1]] * count, axis=1)
            a, b = spectrum[:padded], spectrum[padded:]
            scaled = jnp.concatenate([a * p + b * q, b * p - a * q], axis=0)
            smooth = jnp.dot(inverse_in[...], triple(scaled), preferred_element_type=jnp.float32)
            for f in range(count):
                filtered[slot, f] = smooth[:, f * LANES : (f + 1) * LANES]

            def send_back(device):
                pltpu.make_async_remote_copy(
                    src_ref=filtered.at[slot, :, cell_block(device), :],
                    dst_ref=out_ref.at[:, :, lanes],
                    send_sem=back_send_sem,
                    recv_sem=back_recv_sem,
                    device_id={"lon": device},
                    device_id_type=MESH,
                ).start()

            each(lambda place: send_back(at(place)), lambda place: (at(place) != me) & (place < n // 8))
            if slot == 0:
                pl.when(far)(to_east.start)
            each(lambda place: send_back(at(place)), lambda place: (at(place) != me) & (place >= n // 8))
            out_ref[:, :, lanes] = filtered[slot, :, cell_block(me), :]

    to_east.wait_recv()
    to_west.wait_recv()
    for f in range(count):
        window[f, 2 * cells : 2 * cells + 2, :] = edge_in[2 * f : 2 * f + 2, :]
    for block in range(inner // LANES):
        lanes = slice(block * LANES, (block + 1) * LANES)
        tap = [
            jnp.broadcast_to(weights[m, block : block + 1, :], (cells, LANES)) for m in range(6 + NEAR)
        ]
        for f in range(count):
            total = None
            for m in range(6 + NEAR):
                start = cells + m - 3 - NEAR
                term = tap[m] * window[f, start : start + cells, lanes]
                total = term if total is None else total + term
            out_ref[f, :, polar + block * LANES : polar + (block + 1) * LANES] = total

    to_east.wait_send()
    to_west.wait_send()
    for k in range(slots + 1):

        @pl.when(held == k)
        def _():
            others = out_ref.at[:, :, pl.ds(0, (tiles - k) * LANES)]
            if k > 0:
                drain(others, send_sem)
            drain(others, back_recv_sem)
            for slot in range(k):
                drain(filtered.at[slot, :, pl.ds(0, (n - 1) * cells), :], back_send_sem)


def halves(values):
    high = values.astype(jnp.bfloat16)
    return high, (values - high.astype(jnp.float32)).astype(jnp.bfloat16)


def triple(values):
    high, low = halves(values)
    return jnp.concatenate([high, low, high], axis=0)


def tables(cycle, waves, padded):
    wave = np.arange(padded)
    phase = 2.0 * np.pi / cycle * (np.arange(cycle)[None, :] * wave[:, None] % cycle)
    live = (wave < waves)[:, None]
    forward = np.concatenate([np.cos(phase) * live, np.sin(phase) * live], axis=0)
    theta = 2.0 * np.pi / cycle * wave
    weight = np.where(wave == 0, 1.0, 2.0) / cycle * (wave < waves)
    columns = [np.cos(theta), np.cos(2 * theta), np.cos(3 * theta)]
    columns += [np.sin(theta), np.sin(2 * theta), np.sin(3 * theta), weight, wave]
    per_wave = np.stack(columns, axis=1)
    def stacked(matrix):
        high = matrix.astype(ml_dtypes.bfloat16)
        low = (matrix - high.astype(np.float64)).astype(ml_dtypes.bfloat16)
        return np.concatenate([high, high, low], axis=1)

    return stacked(forward), stacked(forward.T), per_wave.astype(np.float32)


def shards(fields, shifts, fraction, cutoff):
    n = lax.axis_size("lon")
    count, cells, rows = fields.shape
    polar = PLAT * LEV
    inner = rows - 2 * polar
    tiles = 2 * polar // LANES
    cycle = cells * n
    waves = cycle // 6
    slots = max(slot_table(owner_table(n, tiles))) + 1
    padded = -(-waves // 8) * 8
    forward, inverse, per_wave = tables(cycle, waves, padded)
    operands = [fields, shifts.reshape(-1, LANES), fraction.reshape(-1, LANES), cutoff[None]]
    operands += [jnp.asarray(x) for x in (forward, inverse, per_wave)]
    vmem = pl.BlockSpec(memory_space=pltpu.VMEM)
    f32 = jnp.float32
    return pl.pallas_call(
        functools.partial(body, n, polar, waves),
        out_shape=pltpu.VMEM(fields.shape, f32),
        in_specs=[pl.BlockSpec(memory_space=pltpu.HBM)] * 7,
        out_specs=vmem,
        scratch_shapes=[
            pltpu.VMEM((slots, count, cycle, LANES), f32),
            pltpu.VMEM((slots, count, cycle, LANES), f32),
            pltpu.VMEM((count, 3 * cells, inner), f32),
            pltpu.VMEM((8, inner), f32),
            pltpu.VMEM((8, inner), f32),
            pltpu.VMEM((slots, 2, padded, LANES), f32),
            pltpu.VMEM((6 + NEAR, inner // LANES, LANES), f32),
            pltpu.VMEM((rows // LANES, LANES), jnp.int32),
            pltpu.VMEM((rows // LANES, LANES), f32),
            pltpu.VMEM((1, cutoff.shape[0]), jnp.int32),
            pltpu.VMEM(forward.shape, jnp.bfloat16),
            pltpu.VMEM(inverse.shape, jnp.bfloat16),
            pltpu.VMEM(per_wave.shape, f32),
            pltpu.VMEM(fields.shape, f32),
            pltpu.SemaphoreType.DMA((8,)),
            pltpu.SemaphoreType.DMA,
            pltpu.SemaphoreType.DMA((slots, count)),
            pltpu.SemaphoreType.DMA,
            pltpu.SemaphoreType.DMA,
            pltpu.SemaphoreType.DMA((2,)),
            pltpu.SemaphoreType.DMA((2,)),
            pltpu.SemaphoreType.REGULAR((2,)),
        ],
        compiler_params=pltpu.CompilerParams(
            collective_id=0, has_side_effects=True, vmem_limit_bytes=32 * 1024 * 1024
        ),
        name="zonal",
    )(*[pltpu.with_memory_space_constraint(x, pltpu.HBM) for x in operands])


def solution(mesh):
    placed = (P("groups", "lon", None), P("groups"), P("groups"), P("groups"))
    return jax.shard_map(
        shards, mesh=mesh, in_specs=placed, out_specs=P("groups", "lon", None), check_vma=False
    )
```

```python
import functools
import math

import jax
import jax.numpy as jnp
import ml_dtypes
import numpy as np
from jax import lax
from jax.experimental import pallas as pl
from jax.experimental.pallas import tpu as pltpu
from jax.sharding import PartitionSpec as P

LEV = 12
PLAT = 64
LANES = 128
WEST = (11, 8, 9, 7, 10, 6, 4, 5, 3, 2, 1, 0)
EAST = (6, 2, 11, 5, 1, 9, 8, 4, 10, 7, 3, 0)
NEAR = 5
MESH = pl.DeviceIdType.MESH
HIGHEST = lax.Precision.HIGHEST


def stencil(c):
    m = 1.0 - 2.0 * c / 3.0
    square = c * c
    alpha = c - 0.5 * square - 1.5 * square * m
    beta = 0.5 * square - 1.5 * square * m
    gamma = 3.0 * square * m
    small, large = -1.0 / 12.0, 7.0 / 12.0
    face = {-1: small, 0: large, 1: large, 2: small}
    flux = {}
    for j in range(-2, 3):
        total = None
        for scale, tap in ((alpha, face.get(j)), (beta, face.get(j + 1))):
            if tap is not None:
                total = scale * tap if total is None else total + scale * tap
        flux[j] = total + gamma if j == 0 else total
    taps = {}
    for j in range(-3, 3):
        value = flux[j + 1] if j + 1 in flux else None
        if j in flux:
            value = -flux[j] if value is None else value - flux[j]
        taps[j] = value + 1.0 if j == 0 else value
    return taps


def owner_table(n, tiles):
    return [min(t + 1, tiles - 1) * n // 16 for t in range(tiles)]


def slot_table(owners):
    return [owners[:t].count(device) for t, device in enumerate(owners)]


def body(
    n, polar, waves, fields_ref, shifts_ref, fraction_ref, cutoff_ref, forward_ref, inverse_ref, wave_ref,
    out_ref, circles, filtered, window, edge_out, edge_in, factor, weights,
    shifts_in, fraction_in, cutoff_in, forward_in, inverse_in, wave_in, own, local_sem,
    send_sem, recv_sem, back_send_sem, back_recv_sem, halo_send_sem, halo_recv_sem, near_in,
):
    me = lax.axis_index("lon")
    count, cells, rows = fields_ref.shape
    side = polar // LANES
    tiles = 2 * side
    inner = rows - 2 * polar
    cycle = n * cells
    owners = owner_table(n, tiles)
    slot_of = slot_table(owners)
    slots = max(slot_of) + 1

    def lane_of(tile):
        return tile * LANES + inner if tile >= side else tile * LANES

    def picked(slot, value):
        total = jnp.int32(0)
        for t in range(tiles):
            if slot_of[t] == slot:
                total = jnp.where(me == owners[t], value(t), total)
        return total

    def owns(slot):
        return picked(slot, lambda t: 1) == 1

    def my_lanes(slot):
        return pl.ds(pl.multiple_of(picked(slot, lane_of), LANES), LANES)

    held = sum(picked(slot, lambda t: 1) for slot in range(slots))
    east = jnp.where(me + 1 == n, 0, me + 1)
    west = jnp.where(me == 0, n - 1, me - 1)

    def cell_block(device):
        return pl.ds(pl.multiple_of(device * cells, cells), cells)

    def signal(semaphore, device):
        pl.semaphore_signal(semaphore, inc=1, device_id={"lon": device}, device_id_type=MESH)

    def each(act, where):
        def one(device, carry):
            pl.when(where(device))(lambda: act(device))
            return carry

        lax.fori_loop(0, n, one, 0, unroll=n <= 16)

    parts = [pl.ds(0, polar), pl.ds(polar + inner, polar), pl.ds(polar, inner)]
    loads = [
        pltpu.make_async_copy(fields_ref.at[:, :, part], own.at[:, :, part], local_sem.at[7 + k])
        for k, part in enumerate(parts)
    ]
    for load in loads:
        load.start()
    barrier = pltpu.get_barrier_semaphore()
    is_owner = owns(0)
    free = [device for device in range(n) if device not in owners]

    def is_free(device):
        return functools.reduce(jnp.logical_or, [device == other for other in free], False)

    pl.when(is_owner)(lambda: each(lambda place: signal(barrier, n - 1 - place), lambda place: n - 1 - place != me))

    @pl.when(jnp.logical_not(is_owner))
    def _():
        pl.when(me < n - 1)(lambda: signal(barrier, me + 1))
        pl.when(me == 0)(lambda: signal(barrier, n - 1))

    heard = n - len(free) - is_owner.astype(jnp.int32)
    heard += jnp.where(jnp.logical_and(me > 0, is_free(me - 1)), 1, 0)
    if 0 in free:
        heard += jnp.where(me == n - 1, 1, 0)

    def local(source, target, slot):
        return pltpu.make_async_copy(source, target, local_sem.at[slot])

    small = [
        local(shifts_ref, shifts_in, 0),
        local(fraction_ref, fraction_in, 1),
        local(cutoff_ref, cutoff_in, 2),
        local(wave_ref, wave_in, 3),
    ]
    large = [local(forward_ref, forward_in, 4), local(inverse_ref, inverse_in, 5)]
    own_inner = local(
        fields_ref.at[:, :, pl.ds(polar, inner)], window.at[:, pl.ds(cells, cells), :], 6
    )
    for copy in small + large + [own_inner]:
        copy.start()
    edge_out[...] = jnp.zeros_like(edge_out)
    pl.semaphore_wait(barrier, heard)
    pl.when(me > 0)(lambda: signal(near_in.at[0], me - 1))
    pl.when(me == n - 1)(lambda: signal(near_in.at[1], 0))
    loads[0].wait()
    loads[1].wait()

    def send_tile(t):
        lanes = pl.ds(lane_of(t), LANES)
        pltpu.make_async_remote_copy(
            src_ref=own.at[:, :, lanes],
            dst_ref=circles.at[slot_of[t], :, cell_block(me), :],
            send_sem=send_sem,
            recv_sem=recv_sem.at[slot_of[t], 0],
            device_id={"lon": owners[t]},
            device_id_type=MESH,
        ).start()

    for half, order in enumerate((WEST, EAST)):

        @pl.when(lax.div(me * 2, n) == half)
        def _():
            for t in order if len(order) == tiles else range(tiles):
                pl.when(me != owners[t])(lambda t=t: send_tile(t))

    for slot in range(slots):

        @pl.when(owns(slot))
        def _():
            for f in range(count):
                circles[slot, f, cell_block(me), :] = own[f, :, my_lanes(slot)]

    for copy in small + [own_inner, loads[2]]:
        copy.wait()
    for f in range(count):
        edge_out[2 * f : 2 * f + 2, :] = window[f, cells : cells + 2, :]

    to_east = pltpu.make_async_remote_copy(
        src_ref=own.at[:, :, pl.ds(polar, inner)],
        dst_ref=window.at[:, pl.ds(0, cells), :],
        send_sem=halo_send_sem.at[0],
        recv_sem=halo_recv_sem.at[0],
        device_id={"lon": east},
        device_id_type=MESH,
    )
    to_west = pltpu.make_async_remote_copy(
        src_ref=edge_out,
        dst_ref=edge_in,
        send_sem=halo_send_sem.at[1],
        recv_sem=halo_recv_sem.at[1],
        device_id={"lon": west},
        device_id_type=MESH,
    )

    far = me == n - 1
    pl.when(me < n - 1)(lambda: pl.semaphore_wait(near_in.at[0], 1))
    pl.when(jnp.logical_not(far))(to_east.start)
    pl.when(me == 0)(lambda: pl.semaphore_wait(near_in.at[1], 1))
    to_west.start()

    padded = factor.shape[2]

    for slot in range(slots):

        @pl.when(owns(slot))
        def _():
            my_tile = picked(slot, lambda t: t)
            my_row = picked(slot, lambda t: lane_of(t) // LANES)
            c = fraction_in[pl.ds(my_row, 1), :]
            o = stencil(c)
            column = [wave_in[:, m : m + 1] for m in range(8)]
            cos1, cos2, cos3, sin1, sin2, sin3, weight, number = column
            real = o[0] + (o[1] + o[-1]) * cos1 + (o[2] + o[-2]) * cos2 + o[-3] * cos3
            imag = (o[1] - o[-1]) * sin1 + (o[2] - o[-2]) * sin2 - o[-3] * sin3
            turns = number * (shifts_in[pl.ds(my_row, 1), :].astype(jnp.float32) * (1.0 / cycle))
            angle = (turns - jnp.floor(turns)) * (2.0 * math.pi)
            cos_shift = jnp.cos(angle)
            sin_shift = jnp.sin(angle)
            latitudes = cutoff_in.shape[1]
            first = lax.broadcasted_iota(jnp.int32, (latitudes, LANES), 0) * LEV
            row = lax.broadcasted_iota(jnp.int32, (latitudes, LANES), 1) + my_tile * LANES
            chosen = jnp.where((row >= first) & (row < first + LEV), 1.0, 0.0)
            limits = jnp.broadcast_to(cutoff_in[...].astype(jnp.float32), (8, latitudes))
            limit = jnp.dot(limits, chosen, precision=HIGHEST, preferred_element_type=jnp.float32)
            kept = jnp.where(number + 0.5 < limit[0:1], weight, 0.0)
            factor[slot, 0] = kept * (cos_shift * real + sin_shift * imag)
            factor[slot, 1] = kept * (cos_shift * imag - sin_shift * real)

    inner_rows = slice(side, side + inner // LANES)
    inner_taps = stencil(fraction_in[inner_rows, :])
    moves = shifts_in[inner_rows, :]
    is_move = [moves == s for s in range(NEAR + 1)]
    for t in range(-3 - NEAR, 3):
        total = jnp.zeros_like(inner_taps[0])
        for s in range(NEAR + 1):
            if -3 <= t + s <= 2:
                total = jnp.where(is_move[s], inner_taps[t + s], total)
        weights[t + 3 + NEAR] = total
    for copy in large:
        copy.wait()

    def at(place):
        side, rest = lax.div(place, n // 2), lax.rem(place, n // 2)
        return lax.div(rest, 2) * 4 + side * 2 + lax.rem(rest, 2)

    def drain(ref, semaphore):
        pltpu.make_async_copy(ref, ref, semaphore).wait()

    @pl.when(held == 0)
    def _():
        drain(out_ref.at[:, :, pl.ds(0, tiles * LANES)], send_sem)
        pl.when(far)(to_east.start)

    for slot in reversed(range(slots)):

        @pl.when(owns(slot))
        def _():
            lanes = my_lanes(slot)
            drain(circles.at[slot, :, pl.ds(0, (n - 1) * cells), :], recv_sem.at[slot, 0])
            whole = jnp.concatenate([circles[slot, f] for f in range(count)], axis=1)
            spectrum = jnp.dot(forward_in[...], triple(whole), preferred_element_type=jnp.float32)
            p = jnp.concatenate([factor[slot, 0]] * count, axis=1)
            q = jnp.concatenate([factor[slot, 1]] * count, axis=1)
            a, b = spectrum[:padded], spectrum[padded:]
            scaled = jnp.concatenate([a * p + b * q, b * p - a * q], axis=0)
            smooth = jnp.dot(inverse_in[...], triple(scaled), preferred_element_type=jnp.float32)
            for f in range(count):
                filtered[slot, f] = smooth[:, f * LANES : (f + 1) * LANES]

            def send_back(device):
                pltpu.make_async_remote_copy(
                    src_ref=filtered.at[slot, :, cell_block(device), :],
                    dst_ref=out_ref.at[:, :, lanes],
                    send_sem=back_send_sem,
                    recv_sem=back_recv_sem,
                    device_id={"lon": device},
                    device_id_type=MESH,
                ).start()

            each(lambda place: send_back(at(place)), lambda place: (at(place) != me) & (place < n // 8))
            if slot == 0:
                pl.when(far)(to_east.start)
            each(lambda place: send_back(at(place)), lambda place: (at(place) != me) & (place >= n // 8))
            out_ref[:, :, lanes] = filtered[slot, :, cell_block(me), :]

    to_east.wait_recv()
    to_west.wait_recv()
    for f in range(count):
        window[f, 2 * cells : 2 * cells + 2, :] = edge_in[2 * f : 2 * f + 2, :]
    for block in range(inner // LANES):
        lanes = slice(block * LANES, (block + 1) * LANES)
        tap = [
            jnp.broadcast_to(weights[m, block : block + 1, :], (cells, LANES)) for m in range(6 + NEAR)
        ]
        for f in range(count):
            total = None
            for m in range(6 + NEAR):
                start = cells + m - 3 - NEAR
                term = tap[m] * window[f, start : start + cells, lanes]
                total = term if total is None else total + term
            out_ref[f, :, polar + block * LANES : polar + (block + 1) * LANES] = total

    to_east.wait_send()
    to_west.wait_send()
    for k in range(slots + 1):

        @pl.when(held == k)
        def _():
            others = out_ref.at[:, :, pl.ds(0, (tiles - k) * LANES)]
            if k > 0:
                drain(others, send_sem)
            drain(others, back_recv_sem)
            for slot in range(k):
                drain(filtered.at[slot, :, pl.ds(0, (n - 1) * cells), :], back_send_sem)


def halves(values):
    high = values.astype(jnp.bfloat16)
    return high, (values - high.astype(jnp.float32)).astype(jnp.bfloat16)


def triple(values):
    high, low = halves(values)
    return jnp.concatenate([high, low, high], axis=0)


def tables(cycle, waves, padded):
    wave = np.arange(padded)
    phase = 2.0 * np.pi / cycle * (np.arange(cycle)[None, :] * wave[:, None] % cycle)
    live = (wave < waves)[:, None]
    forward = np.concatenate([np.cos(phase) * live, np.sin(phase) * live], axis=0)
    theta = 2.0 * np.pi / cycle * wave
    weight = np.where(wave == 0, 1.0, 2.0) / cycle * (wave < waves)
    columns = [np.cos(theta), np.cos(2 * theta), np.cos(3 * theta)]
    columns += [np.sin(theta), np.sin(2 * theta), np.sin(3 * theta), weight, wave]
    per_wave = np.stack(columns, axis=1)
    def stacked(matrix):
        high = matrix.astype(ml_dtypes.bfloat16)
        low = (matrix - high.astype(np.float64)).astype(ml_dtypes.bfloat16)
        return np.concatenate([high, high, low], axis=1)

    return stacked(forward), stacked(forward.T), per_wave.astype(np.float32)


def shards(fields, shifts, fraction, cutoff):
    n = lax.axis_size("lon")
    count, cells, rows = fields.shape
    polar = PLAT * LEV
    inner = rows - 2 * polar
    tiles = 2 * polar // LANES
    cycle = cells * n
    waves = cycle // 6
    slots = max(slot_table(owner_table(n, tiles))) + 1
    padded = -(-waves // 8) * 8
    forward, inverse, per_wave = tables(cycle, waves, padded)
    operands = [fields, shifts.reshape(-1, LANES), fraction.reshape(-1, LANES), cutoff[None]]
    operands += [jnp.asarray(x) for x in (forward, inverse, per_wave)]
    vmem = pl.BlockSpec(memory_space=pltpu.VMEM)
    f32 = jnp.float32
    return pl.pallas_call(
        functools.partial(body, n, polar, waves),
        out_shape=pltpu.VMEM(fields.shape, f32),
        in_specs=[pl.BlockSpec(memory_space=pltpu.HBM)] * 7,
        out_specs=vmem,
        scratch_shapes=[
            pltpu.VMEM((slots, count, cycle, LANES), f32),
            pltpu.VMEM((slots, count, cycle, LANES), f32),
            pltpu.VMEM((count, 3 * cells, inner), f32),
            pltpu.VMEM((8, inner), f32),
            pltpu.VMEM((8, inner), f32),
            pltpu.VMEM((slots, 2, padded, LANES), f32),
            pltpu.VMEM((6 + NEAR, inner // LANES, LANES), f32),
            pltpu.VMEM((rows // LANES, LANES), jnp.int32),
            pltpu.VMEM((rows // LANES, LANES), f32),
            pltpu.VMEM((1, cutoff.shape[0]), jnp.int32),
            pltpu.VMEM(forward.shape, jnp.bfloat16),
            pltpu.VMEM(inverse.shape, jnp.bfloat16),
            pltpu.VMEM(per_wave.shape, f32),
            pltpu.VMEM(fields.shape, f32),
            pltpu.SemaphoreType.DMA((10,)),
            pltpu.SemaphoreType.DMA,
            pltpu.SemaphoreType.DMA((slots, count)),
            pltpu.SemaphoreType.DMA,
            pltpu.SemaphoreType.DMA,
            pltpu.SemaphoreType.DMA((2,)),
            pltpu.SemaphoreType.DMA((2,)),
            pltpu.SemaphoreType.REGULAR((2,)),
        ],
        compiler_params=pltpu.CompilerParams(
            collective_id=0, has_side_effects=True, vmem_limit_bytes=32 * 1024 * 1024
        ),
        name="zonal",
    )(*[pltpu.with_memory_space_constraint(x, pltpu.HBM) for x in operands])


def solution(mesh):
    placed = (P("groups", "lon", None), P("groups"), P("groups"), P("groups"))
    return jax.shard_map(
        shards, mesh=mesh, in_specs=placed, out_specs=P("groups", "lon", None), check_vma=False
    )
```

```python
import functools
import math

import jax
import jax.numpy as jnp
import ml_dtypes
import numpy as np
from jax import lax
from jax.experimental import pallas as pl
from jax.experimental.pallas import tpu as pltpu
from jax.sharding import PartitionSpec as P

LEV = 12
PLAT = 64
LANES = 128
WEST = (8, 11, 9, 7, 10, 6, 5, 4, 3, 2, 1, 0)
EAST = (6, 11, 2, 5, 1, 9, 8, 4, 7, 10, 3, 0)
NEAR = 5
MESH = pl.DeviceIdType.MESH
HIGHEST = lax.Precision.HIGHEST


def stencil(c):
    m = 1.0 - 2.0 * c / 3.0
    square = c * c
    alpha = c - 0.5 * square - 1.5 * square * m
    beta = 0.5 * square - 1.5 * square * m
    gamma = 3.0 * square * m
    small, large = -1.0 / 12.0, 7.0 / 12.0
    face = {-1: small, 0: large, 1: large, 2: small}
    flux = {}
    for j in range(-2, 3):
        total = None
        for scale, tap in ((alpha, face.get(j)), (beta, face.get(j + 1))):
            if tap is not None:
                total = scale * tap if total is None else total + scale * tap
        flux[j] = total + gamma if j == 0 else total
    taps = {}
    for j in range(-3, 3):
        value = flux[j + 1] if j + 1 in flux else None
        if j in flux:
            value = -flux[j] if value is None else value - flux[j]
        taps[j] = value + 1.0 if j == 0 else value
    return taps


def owner_table(n, tiles):
    return [min(t + 1, tiles - 1) * n // 16 for t in range(tiles)]


def slot_table(owners):
    return [owners[:t].count(device) for t, device in enumerate(owners)]


def body(
    n, polar, waves, fields_ref, shifts_ref, fraction_ref, cutoff_ref, forward_ref, inverse_ref, wave_ref,
    out_ref, circles, filtered, window, edge_out, edge_in, factor, weights,
    shifts_in, fraction_in, cutoff_in, forward_in, inverse_in, wave_in, own, local_sem,
    send_sem, recv_sem, back_send_sem, back_recv_sem, halo_send_sem, halo_recv_sem, near_in,
):
    me = lax.axis_index("lon")
    count, cells, rows = fields_ref.shape
    side = polar // LANES
    tiles = 2 * side
    inner = rows - 2 * polar
    cycle = n * cells
    owners = owner_table(n, tiles)
    slot_of = slot_table(owners)
    slots = max(slot_of) + 1

    def lane_of(tile):
        return tile * LANES + inner if tile >= side else tile * LANES

    def picked(slot, value):
        total = jnp.int32(0)
        for t in range(tiles):
            if slot_of[t] == slot:
                total = jnp.where(me == owners[t], value(t), total)
        return total

    def owns(slot):
        return picked(slot, lambda t: 1) == 1

    def my_lanes(slot):
        return pl.ds(pl.multiple_of(picked(slot, lane_of), LANES), LANES)

    held = sum(picked(slot, lambda t: 1) for slot in range(slots))
    east = jnp.where(me + 1 == n, 0, me + 1)
    west = jnp.where(me == 0, n - 1, me - 1)

    def cell_block(device):
        return pl.ds(pl.multiple_of(device * cells, cells), cells)

    def signal(semaphore, device):
        pl.semaphore_signal(semaphore, inc=1, device_id={"lon": device}, device_id_type=MESH)

    def each(act, where):
        def one(device, carry):
            pl.when(where(device))(lambda: act(device))
            return carry

        lax.fori_loop(0, n, one, 0, unroll=n <= 16)

    parts = [pl.ds(0, polar), pl.ds(polar + inner, polar), pl.ds(polar, inner)]
    loads = [
        pltpu.make_async_copy(fields_ref.at[:, :, part], own.at[:, :, part], local_sem.at[7 + k])
        for k, part in enumerate(parts)
    ]
    for load in loads:
        load.start()
    barrier = pltpu.get_barrier_semaphore()
    is_owner = owns(0)
    free = [device for device in range(n) if device not in owners]

    def is_free(device):
        return functools.reduce(jnp.logical_or, [device == other for other in free], False)

    pl.when(is_owner)(lambda: each(lambda place: signal(barrier, n - 1 - place), lambda place: n - 1 - place != me))

    @pl.when(jnp.logical_not(is_owner))
    def _():
        pl.when(me < n - 1)(lambda: signal(barrier, me + 1))
        pl.when(me == 0)(lambda: signal(barrier, n - 1))

    heard = n - len(free) - is_owner.astype(jnp.int32)
    heard += jnp.where(jnp.logical_and(me > 0, is_free(me - 1)), 1, 0)
    if 0 in free:
        heard += jnp.where(me == n - 1, 1, 0)

    def local(source, target, slot):
        return pltpu.make_async_copy(source, target, local_sem.at[slot])

    small = [
        local(shifts_ref, shifts_in, 0),
        local(fraction_ref, fraction_in, 1),
        local(cutoff_ref, cutoff_in, 2),
        local(wave_ref, wave_in, 3),
    ]
    large = [local(forward_ref, forward_in, 4), local(inverse_ref, inverse_in, 5)]
    own_inner = local(
        fields_ref.at[:, :, pl.ds(polar, inner)], window.at[:, pl.ds(cells, cells), :], 6
    )
    for copy in small + large + [own_inner]:
        copy.start()
    edge_out[...] = jnp.zeros_like(edge_out)
    pl.semaphore_wait(barrier, heard)
    pl.when(me > 0)(lambda: signal(near_in.at[0], me - 1))
    pl.when(me == n - 1)(lambda: signal(near_in.at[1], 0))
    loads[0].wait()
    loads[1].wait()

    def send_tile(t):
        lanes = pl.ds(lane_of(t), LANES)
        pltpu.make_async_remote_copy(
            src_ref=own.at[:, :, lanes],
            dst_ref=circles.at[slot_of[t], :, cell_block(me), :],
            send_sem=send_sem,
            recv_sem=recv_sem.at[slot_of[t], 0],
            device_id={"lon": owners[t]},
            device_id_type=MESH,
        ).start()

    for half, order in enumerate((WEST, EAST)):

        @pl.when(lax.div(me * 2, n) == half)
        def _():
            for t in order if len(order) == tiles else range(tiles):
                pl.when(me != owners[t])(lambda t=t: send_tile(t))

    for slot in range(slots):

        @pl.when(owns(slot))
        def _():
            for f in range(count):
                circles[slot, f, cell_block(me), :] = own[f, :, my_lanes(slot)]

    for copy in small + [own_inner, loads[2]]:
        copy.wait()
    for f in range(count):
        edge_out[2 * f : 2 * f + 2, :] = window[f, cells : cells + 2, :]

    to_east = pltpu.make_async_remote_copy(
        src_ref=own.at[:, :, pl.ds(polar, inner)],
        dst_ref=window.at[:, pl.ds(0, cells), :],
        send_sem=halo_send_sem.at[0],
        recv_sem=halo_recv_sem.at[0],
        device_id={"lon": east},
        device_id_type=MESH,
    )
    to_west = pltpu.make_async_remote_copy(
        src_ref=edge_out,
        dst_ref=edge_in,
        send_sem=halo_send_sem.at[1],
        recv_sem=halo_recv_sem.at[1],
        device_id={"lon": west},
        device_id_type=MESH,
    )

    far = me == n - 1
    pl.when(me < n - 1)(lambda: pl.semaphore_wait(near_in.at[0], 1))
    pl.when(jnp.logical_not(far))(to_east.start)
    pl.when(me == 0)(lambda: pl.semaphore_wait(near_in.at[1], 1))
    to_west.start()

    padded = factor.shape[2]

    for slot in range(slots):

        @pl.when(owns(slot))
        def _():
            my_tile = picked(slot, lambda t: t)
            my_row = picked(slot, lambda t: lane_of(t) // LANES)
            c = fraction_in[pl.ds(my_row, 1), :]
            o = stencil(c)
            column = [wave_in[:, m : m + 1] for m in range(8)]
            cos1, cos2, cos3, sin1, sin2, sin3, weight, number = column
            real = o[0] + (o[1] + o[-1]) * cos1 + (o[2] + o[-2]) * cos2 + o[-3] * cos3
            imag = (o[1] - o[-1]) * sin1 + (o[2] - o[-2]) * sin2 - o[-3] * sin3
            turns = number * (shifts_in[pl.ds(my_row, 1), :].astype(jnp.float32) * (1.0 / cycle))
            angle = (turns - jnp.floor(turns)) * (2.0 * math.pi)
            cos_shift = jnp.cos(angle)
            sin_shift = jnp.sin(angle)
            latitudes = cutoff_in.shape[1]
            first = lax.broadcasted_iota(jnp.int32, (latitudes, LANES), 0) * LEV
            row = lax.broadcasted_iota(jnp.int32, (latitudes, LANES), 1) + my_tile * LANES
            chosen = jnp.where((row >= first) & (row < first + LEV), 1.0, 0.0)
            limits = jnp.broadcast_to(cutoff_in[...].astype(jnp.float32), (8, latitudes))
            limit = jnp.dot(limits, chosen, precision=HIGHEST, preferred_element_type=jnp.float32)
            kept = jnp.where(number + 0.5 < limit[0:1], weight, 0.0)
            factor[slot, 0] = kept * (cos_shift * real + sin_shift * imag)
            factor[slot, 1] = kept * (cos_shift * imag - sin_shift * real)

    inner_rows = slice(side, side + inner // LANES)
    inner_taps = stencil(fraction_in[inner_rows, :])
    moves = shifts_in[inner_rows, :]
    is_move = [moves == s for s in range(NEAR + 1)]
    for t in range(-3 - NEAR, 3):
        total = jnp.zeros_like(inner_taps[0])
        for s in range(NEAR + 1):
            if -3 <= t + s <= 2:
                total = jnp.where(is_move[s], inner_taps[t + s], total)
        weights[t + 3 + NEAR] = total
    for copy in large:
        copy.wait()

    def at(place):
        side, rest = lax.div(place, n // 2), lax.rem(place, n // 2)
        return lax.div(rest, 2) * 4 + side * 2 + lax.rem(rest, 2)

    def drain(ref, semaphore):
        pltpu.make_async_copy(ref, ref, semaphore).wait()

    @pl.when(held == 0)
    def _():
        drain(out_ref.at[:, :, pl.ds(0, tiles * LANES)], send_sem)
        pl.when(far)(to_east.start)

    for slot in reversed(range(slots)):

        @pl.when(owns(slot))
        def _():
            lanes = my_lanes(slot)
            drain(circles.at[slot, :, pl.ds(0, (n - 1) * cells), :], recv_sem.at[slot, 0])
            whole = jnp.concatenate([circles[slot, f] for f in range(count)], axis=1)
            spectrum = jnp.dot(forward_in[...], triple(whole), preferred_element_type=jnp.float32)
            p = jnp.concatenate([factor[slot, 0]] * count, axis=1)
            q = jnp.concatenate([factor[slot, 1]] * count, axis=1)
            a, b = spectrum[:padded], spectrum[padded:]
            scaled = jnp.concatenate([a * p + b * q, b * p - a * q], axis=0)
            smooth = jnp.dot(inverse_in[...], triple(scaled), preferred_element_type=jnp.float32)
            for f in range(count):
                filtered[slot, f] = smooth[:, f * LANES : (f + 1) * LANES]

            def send_back(device):
                pltpu.make_async_remote_copy(
                    src_ref=filtered.at[slot, :, cell_block(device), :],
                    dst_ref=out_ref.at[:, :, lanes],
                    send_sem=back_send_sem,
                    recv_sem=back_recv_sem,
                    device_id={"lon": device},
                    device_id_type=MESH,
                ).start()

            each(lambda place: send_back(at(place)), lambda place: (at(place) != me) & (place < n // 8))
            if slot == 0:
                pl.when(far)(to_east.start)
            each(lambda place: send_back(at(place)), lambda place: (at(place) != me) & (place >= n // 8))
            out_ref[:, :, lanes] = filtered[slot, :, cell_block(me), :]

    to_east.wait_recv()
    to_west.wait_recv()
    for f in range(count):
        window[f, 2 * cells : 2 * cells + 2, :] = edge_in[2 * f : 2 * f + 2, :]
    for block in range(inner // LANES):
        lanes = slice(block * LANES, (block + 1) * LANES)
        tap = [
            jnp.broadcast_to(weights[m, block : block + 1, :], (cells, LANES)) for m in range(6 + NEAR)
        ]
        for f in range(count):
            total = None
            for m in range(6 + NEAR):
                start = cells + m - 3 - NEAR
                term = tap[m] * window[f, start : start + cells, lanes]
                total = term if total is None else total + term
            out_ref[f, :, polar + block * LANES : polar + (block + 1) * LANES] = total

    to_east.wait_send()
    to_west.wait_send()
    for k in range(slots + 1):

        @pl.when(held == k)
        def _():
            others = out_ref.at[:, :, pl.ds(0, (tiles - k) * LANES)]
            if k > 0:
                drain(others, send_sem)
            drain(others, back_recv_sem)
            for slot in range(k):
                drain(filtered.at[slot, :, pl.ds(0, (n - 1) * cells), :], back_send_sem)


def halves(values):
    high = values.astype(jnp.bfloat16)
    return high, (values - high.astype(jnp.float32)).astype(jnp.bfloat16)


def triple(values):
    high, low = halves(values)
    return jnp.concatenate([high, low, high], axis=0)


def tables(cycle, waves, padded):
    wave = np.arange(padded)
    phase = 2.0 * np.pi / cycle * (np.arange(cycle)[None, :] * wave[:, None] % cycle)
    live = (wave < waves)[:, None]
    forward = np.concatenate([np.cos(phase) * live, np.sin(phase) * live], axis=0)
    theta = 2.0 * np.pi / cycle * wave
    weight = np.where(wave == 0, 1.0, 2.0) / cycle * (wave < waves)
    columns = [np.cos(theta), np.cos(2 * theta), np.cos(3 * theta)]
    columns += [np.sin(theta), np.sin(2 * theta), np.sin(3 * theta), weight, wave]
    per_wave = np.stack(columns, axis=1)
    def stacked(matrix):
        high = matrix.astype(ml_dtypes.bfloat16)
        low = (matrix - high.astype(np.float64)).astype(ml_dtypes.bfloat16)
        return np.concatenate([high, high, low], axis=1)

    return stacked(forward), stacked(forward.T), per_wave.astype(np.float32)


def shards(fields, shifts, fraction, cutoff):
    n = lax.axis_size("lon")
    count, cells, rows = fields.shape
    polar = PLAT * LEV
    inner = rows - 2 * polar
    tiles = 2 * polar // LANES
    cycle = cells * n
    waves = cycle // 6
    slots = max(slot_table(owner_table(n, tiles))) + 1
    padded = -(-waves // 8) * 8
    forward, inverse, per_wave = tables(cycle, waves, padded)
    operands = [fields, shifts.reshape(-1, LANES), fraction.reshape(-1, LANES), cutoff[None]]
    operands += [jnp.asarray(x) for x in (forward, inverse, per_wave)]
    vmem = pl.BlockSpec(memory_space=pltpu.VMEM)
    f32 = jnp.float32
    return pl.pallas_call(
        functools.partial(body, n, polar, waves),
        out_shape=pltpu.VMEM(fields.shape, f32),
        in_specs=[pl.BlockSpec(memory_space=pltpu.HBM)] * 7,
        out_specs=vmem,
        scratch_shapes=[
            pltpu.VMEM((slots, count, cycle, LANES), f32),
            pltpu.VMEM((slots, count, cycle, LANES), f32),
            pltpu.VMEM((count, 3 * cells, inner), f32),
            pltpu.VMEM((8, inner), f32),
            pltpu.VMEM((8, inner), f32),
            pltpu.VMEM((slots, 2, padded, LANES), f32),
            pltpu.VMEM((6 + NEAR, inner // LANES, LANES), f32),
            pltpu.VMEM((rows // LANES, LANES), jnp.int32),
            pltpu.VMEM((rows // LANES, LANES), f32),
            pltpu.VMEM((1, cutoff.shape[0]), jnp.int32),
            pltpu.VMEM(forward.shape, jnp.bfloat16),
            pltpu.VMEM(inverse.shape, jnp.bfloat16),
            pltpu.VMEM(per_wave.shape, f32),
            pltpu.VMEM(fields.shape, f32),
            pltpu.SemaphoreType.DMA((10,)),
            pltpu.SemaphoreType.DMA,
            pltpu.SemaphoreType.DMA((slots, count)),
            pltpu.SemaphoreType.DMA,
            pltpu.SemaphoreType.DMA,
            pltpu.SemaphoreType.DMA((2,)),
            pltpu.SemaphoreType.DMA((2,)),
            pltpu.SemaphoreType.REGULAR((2,)),
        ],
        compiler_params=pltpu.CompilerParams(
            collective_id=0, has_side_effects=True, vmem_limit_bytes=32 * 1024 * 1024
        ),
        name="zonal",
    )(*[pltpu.with_memory_space_constraint(x, pltpu.HBM) for x in operands])


def solution(mesh):
    placed = (P("groups", "lon", None), P("groups"), P("groups"), P("groups"))
    return jax.shard_map(
        shards, mesh=mesh, in_specs=placed, out_specs=P("groups", "lon", None), check_vma=False
    )
```

```python
import functools
import math

import jax
import jax.numpy as jnp
import ml_dtypes
import numpy as np
from jax import lax
from jax.experimental import pallas as pl
from jax.experimental.pallas import tpu as pltpu
from jax.sharding import PartitionSpec as P

LEV = 12
PLAT = 64
LANES = 128
WEST = (11, 8, 9, 7, 10, 6, 4, 5, 3, 2, 1, 0)
EAST = (6, 2, 11, 5, 1, 9, 8, 4, 10, 7, 3, 0)
NEAR = 5
MESH = pl.DeviceIdType.MESH
HIGHEST = lax.Precision.HIGHEST


def stencil(c):
    m = 1.0 - 2.0 * c / 3.0
    square = c * c
    alpha = c - 0.5 * square - 1.5 * square * m
    beta = 0.5 * square - 1.5 * square * m
    gamma = 3.0 * square * m
    small, large = -1.0 / 12.0, 7.0 / 12.0
    face = {-1: small, 0: large, 1: large, 2: small}
    flux = {}
    for j in range(-2, 3):
        total = None
        for scale, tap in ((alpha, face.get(j)), (beta, face.get(j + 1))):
            if tap is not None:
                total = scale * tap if total is None else total + scale * tap
        flux[j] = total + gamma if j == 0 else total
    taps = {}
    for j in range(-3, 3):
        value = flux[j + 1] if j + 1 in flux else None
        if j in flux:
            value = -flux[j] if value is None else value - flux[j]
        taps[j] = value + 1.0 if j == 0 else value
    return taps


def owner_table(n, tiles):
    return [min(t + 1, tiles - 1) * n // 16 for t in range(tiles)]


def slot_table(owners):
    return [owners[:t].count(device) for t, device in enumerate(owners)]


def body(
    n, polar, waves, fields_ref, shifts_ref, fraction_ref, cutoff_ref, forward_ref, inverse_ref, wave_ref,
    out_ref, circles, filtered, window, edge_out, edge_in, factor, weights,
    shifts_in, fraction_in, cutoff_in, forward_in, inverse_in, wave_in, own, local_sem,
    send_sem, recv_sem, back_send_sem, back_recv_sem, halo_send_sem, halo_recv_sem, near_in,
):
    me = lax.axis_index("lon")
    count, cells, rows = fields_ref.shape
    side = polar // LANES
    tiles = 2 * side
    inner = rows - 2 * polar
    cycle = n * cells
    owners = owner_table(n, tiles)
    slot_of = slot_table(owners)
    slots = max(slot_of) + 1

    def lane_of(tile):
        return tile * LANES + inner if tile >= side else tile * LANES

    def picked(slot, value):
        total = jnp.int32(0)
        for t in range(tiles):
            if slot_of[t] == slot:
                total = jnp.where(me == owners[t], value(t), total)
        return total

    def owns(slot):
        return picked(slot, lambda t: 1) == 1

    def my_lanes(slot):
        return pl.ds(pl.multiple_of(picked(slot, lane_of), LANES), LANES)

    held = sum(picked(slot, lambda t: 1) for slot in range(slots))
    east = jnp.where(me + 1 == n, 0, me + 1)
    west = jnp.where(me == 0, n - 1, me - 1)

    def cell_block(device):
        return pl.ds(pl.multiple_of(device * cells, cells), cells)

    def signal(semaphore, device):
        pl.semaphore_signal(semaphore, inc=1, device_id={"lon": device}, device_id_type=MESH)

    def each(act, where):
        def one(device, carry):
            pl.when(where(device))(lambda: act(device))
            return carry

        lax.fori_loop(0, n, one, 0, unroll=n <= 16)

    parts = [pl.ds(0, polar), pl.ds(polar + inner, polar), pl.ds(polar, inner)]
    loads = [
        pltpu.make_async_copy(fields_ref.at[:, :, part], own.at[:, :, part], local_sem.at[7 + k])
        for k, part in enumerate(parts)
    ]
    for load in loads:
        load.start()
    barrier = pltpu.get_barrier_semaphore()
    is_owner = owns(0)
    free = [device for device in range(n) if device not in owners]

    def is_free(device):
        return functools.reduce(jnp.logical_or, [device == other for other in free], False)

    pl.when(is_owner)(lambda: each(lambda place: signal(barrier, n - 1 - place), lambda place: n - 1 - place != me))

    @pl.when(jnp.logical_not(is_owner))
    def _():
        pl.when(me < n - 1)(lambda: signal(barrier, me + 1))
        pl.when(me == 0)(lambda: signal(barrier, n - 1))

    heard = n - len(free) - is_owner.astype(jnp.int32)
    heard += jnp.where(jnp.logical_and(me > 0, is_free(me - 1)), 1, 0)
    if 0 in free:
        heard += jnp.where(me == n - 1, 1, 0)

    def local(source, target, slot):
        return pltpu.make_async_copy(source, target, local_sem.at[slot])

    small = [
        local(shifts_ref, shifts_in, 0),
        local(fraction_ref, fraction_in, 1),
        local(cutoff_ref, cutoff_in, 2),
        local(wave_ref, wave_in, 3),
    ]
    large = [local(forward_ref, forward_in, 4), local(inverse_ref, inverse_in, 5)]
    own_inner = local(
        fields_ref.at[:, :, pl.ds(polar, inner)], window.at[:, pl.ds(cells, cells), :], 6
    )
    edge_out[...] = jnp.zeros_like(edge_out)
    pl.semaphore_wait(barrier, heard)
    pl.when(me > 0)(lambda: signal(near_in.at[0], me - 1))
    pl.when(me == n - 1)(lambda: signal(near_in.at[1], 0))
    for copy in small + large + [own_inner]:
        copy.start()
    loads[0].wait()
    loads[1].wait()

    def send_tile(t):
        lanes = pl.ds(lane_of(t), LANES)
        pltpu.make_async_remote_copy(
            src_ref=own.at[:, :, lanes],
            dst_ref=circles.at[slot_of[t], :, cell_block(me), :],
            send_sem=send_sem,
            recv_sem=recv_sem.at[slot_of[t], 0],
            device_id={"lon": owners[t]},
            device_id_type=MESH,
        ).start()

    for half, order in enumerate((WEST, EAST)):

        @pl.when(lax.div(me * 2, n) == half)
        def _():
            for t in order if len(order) == tiles else range(tiles):
                pl.when(me != owners[t])(lambda t=t: send_tile(t))

    for slot in range(slots):

        @pl.when(owns(slot))
        def _():
            for f in range(count):
                circles[slot, f, cell_block(me), :] = own[f, :, my_lanes(slot)]

    for copy in small + [own_inner, loads[2]]:
        copy.wait()
    for f in range(count):
        edge_out[2 * f : 2 * f + 2, :] = window[f, cells : cells + 2, :]

    to_east = pltpu.make_async_remote_copy(
        src_ref=own.at[:, :, pl.ds(polar, inner)],
        dst_ref=window.at[:, pl.ds(0, cells), :],
        send_sem=halo_send_sem.at[0],
        recv_sem=halo_recv_sem.at[0],
        device_id={"lon": east},
        device_id_type=MESH,
    )
    to_west = pltpu.make_async_remote_copy(
        src_ref=edge_out,
        dst_ref=edge_in,
        send_sem=halo_send_sem.at[1],
        recv_sem=halo_recv_sem.at[1],
        device_id={"lon": west},
        device_id_type=MESH,
    )

    far = me == n - 1
    pl.when(me < n - 1)(lambda: pl.semaphore_wait(near_in.at[0], 1))
    pl.when(jnp.logical_not(far))(to_east.start)
    pl.when(me == 0)(lambda: pl.semaphore_wait(near_in.at[1], 1))
    to_west.start()

    padded = factor.shape[2]

    for slot in range(slots):

        @pl.when(owns(slot))
        def _():
            my_tile = picked(slot, lambda t: t)
            my_row = picked(slot, lambda t: lane_of(t) // LANES)
            c = fraction_in[pl.ds(my_row, 1), :]
            o = stencil(c)
            column = [wave_in[:, m : m + 1] for m in range(8)]
            cos1, cos2, cos3, sin1, sin2, sin3, weight, number = column
            real = o[0] + (o[1] + o[-1]) * cos1 + (o[2] + o[-2]) * cos2 + o[-3] * cos3
            imag = (o[1] - o[-1]) * sin1 + (o[2] - o[-2]) * sin2 - o[-3] * sin3
            turns = number * (shifts_in[pl.ds(my_row, 1), :].astype(jnp.float32) * (1.0 / cycle))
            angle = (turns - jnp.floor(turns)) * (2.0 * math.pi)
            cos_shift = jnp.cos(angle)
            sin_shift = jnp.sin(angle)
            latitudes = cutoff_in.shape[1]
            first = lax.broadcasted_iota(jnp.int32, (latitudes, LANES), 0) * LEV
            row = lax.broadcasted_iota(jnp.int32, (latitudes, LANES), 1) + my_tile * LANES
            chosen = jnp.where((row >= first) & (row < first + LEV), 1.0, 0.0)
            limits = jnp.broadcast_to(cutoff_in[...].astype(jnp.float32), (8, latitudes))
            limit = jnp.dot(limits, chosen, precision=HIGHEST, preferred_element_type=jnp.float32)
            kept = jnp.where(number + 0.5 < limit[0:1], weight, 0.0)
            factor[slot, 0] = kept * (cos_shift * real + sin_shift * imag)
            factor[slot, 1] = kept * (cos_shift * imag - sin_shift * real)

    inner_rows = slice(side, side + inner // LANES)
    inner_taps = stencil(fraction_in[inner_rows, :])
    moves = shifts_in[inner_rows, :]
    is_move = [moves == s for s in range(NEAR + 1)]
    for t in range(-3 - NEAR, 3):
        total = jnp.zeros_like(inner_taps[0])
        for s in range(NEAR + 1):
            if -3 <= t + s <= 2:
                total = jnp.where(is_move[s], inner_taps[t + s], total)
        weights[t + 3 + NEAR] = total
    for copy in large:
        copy.wait()

    def at(place):
        side, rest = lax.div(place, n // 2), lax.rem(place, n // 2)
        return lax.div(rest, 2) * 4 + side * 2 + lax.rem(rest, 2)

    def drain(ref, semaphore):
        pltpu.make_async_copy(ref, ref, semaphore).wait()

    @pl.when(held == 0)
    def _():
        drain(out_ref.at[:, :, pl.ds(0, tiles * LANES)], send_sem)
        pl.when(far)(to_east.start)

    for slot in reversed(range(slots)):

        @pl.when(owns(slot))
        def _():
            lanes = my_lanes(slot)
            drain(circles.at[slot, :, pl.ds(0, (n - 1) * cells), :], recv_sem.at[slot, 0])
            whole = jnp.concatenate([circles[slot, f] for f in range(count)], axis=1)
            spectrum = jnp.dot(forward_in[...], triple(whole), preferred_element_type=jnp.float32)
            p = jnp.concatenate([factor[slot, 0]] * count, axis=1)
            q = jnp.concatenate([factor[slot, 1]] * count, axis=1)
            a, b = spectrum[:padded], spectrum[padded:]
            scaled = jnp.concatenate([a * p + b * q, b * p - a * q], axis=0)
            smooth = jnp.dot(inverse_in[...], triple(scaled), preferred_element_type=jnp.float32)
            for f in range(count):
                filtered[slot, f] = smooth[:, f * LANES : (f + 1) * LANES]

            def send_back(device):
                pltpu.make_async_remote_copy(
                    src_ref=filtered.at[slot, :, cell_block(device), :],
                    dst_ref=out_ref.at[:, :, lanes],
                    send_sem=back_send_sem,
                    recv_sem=back_recv_sem,
                    device_id={"lon": device},
                    device_id_type=MESH,
                ).start()

            each(lambda place: send_back(at(place)), lambda place: (at(place) != me) & (place < n // 8))
            if slot == 0:
                pl.when(far)(to_east.start)
            each(lambda place: send_back(at(place)), lambda place: (at(place) != me) & (place >= n // 8))
            out_ref[:, :, lanes] = filtered[slot, :, cell_block(me), :]

    to_east.wait_recv()
    to_west.wait_recv()
    for f in range(count):
        window[f, 2 * cells : 2 * cells + 2, :] = edge_in[2 * f : 2 * f + 2, :]
    for block in range(inner // LANES):
        lanes = slice(block * LANES, (block + 1) * LANES)
        tap = [
            jnp.broadcast_to(weights[m, block : block + 1, :], (cells, LANES)) for m in range(6 + NEAR)
        ]
        for f in range(count):
            total = None
            for m in range(6 + NEAR):
                start = cells + m - 3 - NEAR
                term = tap[m] * window[f, start : start + cells, lanes]
                total = term if total is None else total + term
            out_ref[f, :, polar + block * LANES : polar + (block + 1) * LANES] = total

    to_east.wait_send()
    to_west.wait_send()
    for k in range(slots + 1):

        @pl.when(held == k)
        def _():
            others = out_ref.at[:, :, pl.ds(0, (tiles - k) * LANES)]
            if k > 0:
                drain(others, send_sem)
            drain(others, back_recv_sem)
            for slot in range(k):
                drain(filtered.at[slot, :, pl.ds(0, (n - 1) * cells), :], back_send_sem)


def halves(values):
    high = values.astype(jnp.bfloat16)
    return high, (values - high.astype(jnp.float32)).astype(jnp.bfloat16)


def triple(values):
    high, low = halves(values)
    return jnp.concatenate([high, low, high], axis=0)


def tables(cycle, waves, padded):
    wave = np.arange(padded)
    phase = 2.0 * np.pi / cycle * (np.arange(cycle)[None, :] * wave[:, None] % cycle)
    live = (wave < waves)[:, None]
    forward = np.concatenate([np.cos(phase) * live, np.sin(phase) * live], axis=0)
    theta = 2.0 * np.pi / cycle * wave
    weight = np.where(wave == 0, 1.0, 2.0) / cycle * (wave < waves)
    columns = [np.cos(theta), np.cos(2 * theta), np.cos(3 * theta)]
    columns += [np.sin(theta), np.sin(2 * theta), np.sin(3 * theta), weight, wave]
    per_wave = np.stack(columns, axis=1)
    def stacked(matrix):
        high = matrix.astype(ml_dtypes.bfloat16)
        low = (matrix - high.astype(np.float64)).astype(ml_dtypes.bfloat16)
        return np.concatenate([high, high, low], axis=1)

    return stacked(forward), stacked(forward.T), per_wave.astype(np.float32)


def shards(fields, shifts, fraction, cutoff):
    n = lax.axis_size("lon")
    count, cells, rows = fields.shape
    polar = PLAT * LEV
    inner = rows - 2 * polar
    tiles = 2 * polar // LANES
    cycle = cells * n
    waves = cycle // 6
    slots = max(slot_table(owner_table(n, tiles))) + 1
    padded = -(-waves // 8) * 8
    forward, inverse, per_wave = tables(cycle, waves, padded)
    operands = [fields, shifts.reshape(-1, LANES), fraction.reshape(-1, LANES), cutoff[None]]
    operands += [jnp.asarray(x) for x in (forward, inverse, per_wave)]
    vmem = pl.BlockSpec(memory_space=pltpu.VMEM)
    f32 = jnp.float32
    return pl.pallas_call(
        functools.partial(body, n, polar, waves),
        out_shape=pltpu.VMEM(fields.shape, f32),
        in_specs=[pl.BlockSpec(memory_space=pltpu.HBM)] * 7,
        out_specs=vmem,
        scratch_shapes=[
            pltpu.VMEM((slots, count, cycle, LANES), f32),
            pltpu.VMEM((slots, count, cycle, LANES), f32),
            pltpu.VMEM((count, 3 * cells, inner), f32),
            pltpu.VMEM((8, inner), f32),
            pltpu.VMEM((8, inner), f32),
            pltpu.VMEM((slots, 2, padded, LANES), f32),
            pltpu.VMEM((6 + NEAR, inner // LANES, LANES), f32),
            pltpu.VMEM((rows // LANES, LANES), jnp.int32),
            pltpu.VMEM((rows // LANES, LANES), f32),
            pltpu.VMEM((1, cutoff.shape[0]), jnp.int32),
            pltpu.VMEM(forward.shape, jnp.bfloat16),
            pltpu.VMEM(inverse.shape, jnp.bfloat16),
            pltpu.VMEM(per_wave.shape, f32),
            pltpu.VMEM(fields.shape, f32),
            pltpu.SemaphoreType.DMA((10,)),
            pltpu.SemaphoreType.DMA,
            pltpu.SemaphoreType.DMA((slots, count)),
            pltpu.SemaphoreType.DMA,
            pltpu.SemaphoreType.DMA,
            pltpu.SemaphoreType.DMA((2,)),
            pltpu.SemaphoreType.DMA((2,)),
            pltpu.SemaphoreType.REGULAR((2,)),
        ],
        compiler_params=pltpu.CompilerParams(
            collective_id=0, has_side_effects=True, vmem_limit_bytes=32 * 1024 * 1024
        ),
        name="zonal",
    )(*[pltpu.with_memory_space_constraint(x, pltpu.HBM) for x in operands])


def solution(mesh):
    placed = (P("groups", "lon", None), P("groups"), P("groups"), P("groups"))
    return jax.shard_map(
        shards, mesh=mesh, in_specs=placed, out_specs=P("groups", "lon", None), check_vma=False
    )
```
